32 devices in a mesh: img: 4 (over y, x), tpl: 8 (over z, core).
Axes of the slice: x: 2, y: 2, z: 4, core: 2. Of those that a mesh axis runs over, the one named last changes fastest.
Arguments:
- images: bfloat16 [6144, 2048], P(('img', 'tpl')), may hold values from -320 to 320
- templates: bfloat16 [3072, 2048], P('tpl'), may hold values from -0.62 to 0.62
- class_exponent: int32 [8], replicated, may hold values from 0 to 5
- class_mask: int32 [6144, 8], P('img'), may hold values from 0 to 1, as said below
Outputs:
- new_templates: float32 [3072, 2048], P('tpl', 'img')
- log_evidence: float32 [6144], P('img')
The draws below stay inside these ranges and needn't reach their ends.
Inputs may be any that keep to these rules, and one draw needn't show every extreme that they name: `class_mask`: every image is compared with at least one class.
All inputs are finite; a program needn't handle non-finite values.
Results may differ from the reference program's by a relative error of at most 0.0023.
Values may be sent and summed in bfloat16 or wider, within the bound.
A program may use at most 64 MiB of HBM per device.

```python
import math
import jax
import jax.numpy as jnp
from jax import lax

F = 2048
CLASSES = 8
IMG_DEV = 1536
IMAGES = 6144
TEMPLATES = 3072
N_IMG = 4


def shared_draw(key):
    key_base = jax.random.fold_in(key, 101)
    key_scale = jax.random.fold_in(key, 102)
    key_pics = jax.random.fold_in(key, 103)
    key_rows = jax.random.fold_in(key, 104)
    base = jnp.clip(jax.random.normal(key_base, (TEMPLATES, F), jnp.float32), -5.0, 5.0)
    tpl_scale = jnp.exp(jax.random.uniform(key_scale, (TEMPLATES, 1), jnp.float32, math.log(0.03), math.log(0.1)))
    pictures = jnp.clip(jax.random.normal(key_pics, (IMAGES, F), jnp.float32), -5.0, 5.0)
    pic_scale = jnp.exp(jax.random.uniform(key_rows, (IMAGES, 1), jnp.float32, math.log(0.5), math.log(2.0)))
    return (base, base * tpl_scale, pictures * pic_scale)


def aligned_draw(base, tmpl, pictures):
    picks = (jnp.arange(8, dtype=jnp.int32) * (TEMPLATES // 8)).astype(jnp.int32)
    rows = base[picks]
    signs = jnp.where(rows >= 0.0, 1.0, -1.0)
    leading = 0.12 * signs * (1.0 + jnp.minimum(jnp.abs(rows), 4.0))
    tmpl = tmpl.at[picks].set(leading).at[picks + 1].set(1.02 * leading)
    targets = (jnp.arange(8, dtype=jnp.int32) * (IMAGES // 8) + 3).astype(jnp.int32)
    factors = jnp.array([6.0, 8.0, 10.0, 12.0, 6.0, 8.0, 10.0, 12.0], jnp.float32)
    norms = jnp.sum(leading * leading, axis=1, keepdims=True)
    gains = 40.0 * factors[:, None] / norms
    pictures = pictures.at[targets].set(gains * leading)
    return (tmpl, pictures)


def draw_images(key, part):
    base, tmpl, pictures = shared_draw(key)
    tmpl, pictures = aligned_draw(base, tmpl, pictures)
    return pictures.astype(jnp.bfloat16)


def draw_templates(key, part):
    base, tmpl, pictures = shared_draw(key)
    tmpl, pictures = aligned_draw(base, tmpl, pictures)
    return tmpl.astype(jnp.bfloat16)


def draw_class_mask(key, part):
    key_bits = jax.random.fold_in(key, 201)
    key_force = jax.random.fold_in(key, 202)
    chosen = jax.random.randint(key_bits, (IMAGES, CLASSES), 0, 4) > 0
    forced = jax.random.randint(key_force, (IMAGES,), 0, CLASSES)
    forced_hit = jnp.arange(CLASSES, dtype=jnp.int32)[None, :] == forced[:, None]
    return jnp.logical_or(chosen, forced_hit).astype(jnp.int32)


def plant(drawn, key, least, high):
    longest = drawn.shape.index(max(drawn.shape))
    spots = []
    for shift in (0, 1):
        where = [jax.random.randint(jax.random.fold_in(key, axis), (), 0, length) for axis, length in enumerate(drawn.shape)]
        where[longest] = (where[longest] + shift) % drawn.shape[longest]
        spots.append(tuple(where))
    return drawn.at[spots[0]].set(least).at[spots[1]].set(high)


def setup_inputs(seed: int = 0) -> dict:
    keys = jax.random.split(jax.random.key(seed), 5)
    return {
        "images": draw_images(jax.random.fold_in(keys[4], 71), 0),
        "templates": draw_templates(jax.random.fold_in(keys[4], 71), 0),
        "class_exponent": plant(jax.random.randint(keys[2], (CLASSES,), 0, 6), jax.random.fold_in(keys[2], 1), 0, 5).astype(jnp.int32),
        "class_mask": draw_class_mask(jax.random.fold_in(keys[4], 71), 0),
    }


floor_score = -1.0e30


def reference(images, templates, class_exponent, class_mask):
    total_rows = templates.shape[0]
    per_class = total_rows // CLASSES
    template_f32 = templates.astype(jnp.float32)
    squared_norm = jnp.sum(template_f32 * template_f32, axis=1)
    owner = (jnp.arange(total_rows, dtype=jnp.int32) // per_class).astype(jnp.int32)
    inverse_temp = 0.5 * jnp.exp2(0.5 * class_exponent.astype(jnp.float32))
    beta = inverse_temp[owner]
    picture_blocks = images.reshape(N_IMG, IMG_DEV, F)
    mask_blocks = class_mask.reshape(N_IMG, IMG_DEV, CLASSES)

    def block_step(carry, item):
        pictures, allow_rows = item
        raw = jnp.dot(pictures, templates.T, preferred_element_type=jnp.float32)
        scores = beta[None, :] * (raw - 0.5 * squared_norm[None, :])
        allowed = allow_rows[:, owner] > 0
        top = jnp.max(jnp.where(allowed, scores, floor_score), axis=1, keepdims=True)
        expo = jnp.where(allowed, jnp.exp(scores - top), 0.0)
        totals = jnp.sum(expo, axis=1, keepdims=True)
        posterior = expo / totals
        weighted = carry[0] + jnp.dot(posterior.astype(jnp.bfloat16).T, pictures, preferred_element_type=jnp.float32)
        occupancy = carry[1] + jnp.sum(posterior, axis=0)
        return (weighted, occupancy), (top + jnp.log(totals))[:, 0]

    start = (jnp.zeros((total_rows, F), jnp.float32), jnp.zeros((total_rows,), jnp.float32))
    (weighted, occupancy), evidence = lax.scan(block_step, start, (picture_blocks, mask_blocks))
    new_templates = (weighted + template_f32) / (occupancy[:, None] + 1.0)
    return new_templates, evidence.reshape(-1)
```

```python
import functools

import jax
import jax.numpy as jnp
from jax import lax
from jax.experimental import pallas as pl
from jax.experimental.pallas import tpu as pltpu
from jax.sharding import PartitionSpec as P

MESH = pl.DeviceIdType.MESH
floor_score = -1e30


def kernel(
    n_img, n_tpl, parts, x_ref, t_hbm, power_ref, mask_hbm, out_ref, le_ref,
    t_ref, mask_ref, loads, imgs, allow, le_row, e_ref, post_ref, st, acc, own, sbuf, rbuf, sqn, occ, obuf, orecv,
    img_send, img_recv, st_send, st_recv, rs_send, rs_recv, oc_send, oc_recv,
    et_ref, e_end, post_end, sqn_end, occ_end, own_end, sbuf_end, rbuf_end, zsend, zrecv, obuf_end, orecv_end,
    et_send, et_recv, est_send, ers_send, ers_recv, z_send, z_recv, hand_send, hand_recv,
):
    chips = n_tpl // 2
    last = chips - 1
    hubs = chips >= 4
    rows, feats = x_ref.shape
    cols = feats // n_img
    me_i, me_t = lax.axis_index("img"), lax.axis_index("tpl")
    chip, core = lax.div(me_t, 2), lax.rem(me_t, 2)
    sibling = 2 * chip + 1 - core
    side = lax.div(2 * chip, chips)
    inward = 1 - 2 * side
    rank = chip + side * (last - 2 * chip)
    inner, outer = me_t + 2 * inward, me_t - 2 * inward
    is_end = jnp.logical_and(rank == 0, hubs)
    is_hub = jnp.logical_and(rank == 1, hubs)
    skip = jnp.where(is_end, 1, 0)
    end_slot = outer

    def absent(q, who):
        if not hubs:
            return False
        low = jnp.logical_and(q == 1, who == 0)
        return jnp.logical_or(low, jnp.logical_and(q == last - 1, who == last))

    def tpl_peer(off):
        return lax.rem(me_t + off, n_tpl)

    def img_peer(off):
        return lax.rem(me_i + off, n_img)

    barrier = pltpu.get_barrier_semaphore()
    for off in range(1, n_tpl):
        pl.semaphore_signal(barrier, inc=1, device_id={"tpl": tpl_peer(off)}, device_id_type=MESH)
    for off in range(1, n_img):
        pl.semaphore_signal(barrier, inc=1, device_id={"img": img_peer(off)}, device_id_type=MESH)
    load_t = pltpu.make_async_copy(t_hbm, t_ref, loads.at[0])
    load_x = pltpu.make_async_copy(x_ref, imgs.at[me_t], loads.at[1])
    load_mask = pltpu.make_async_copy(mask_hbm, mask_ref, loads.at[2])
    for load in (load_t, load_x, load_mask):
        load.start()
    pl.semaphore_wait(barrier, n_tpl - 1 + n_img - 1)

    size = rows // parts
    tpl_rows = t_ref.shape[0]
    quarter = tpl_rows // n_img
    t_parts = 2 if quarter % 32 == 0 else 1
    t_size = quarter // t_parts

    def image_copy(src, block, k, way, to):
        piece = pl.ds(k * size, size)
        return pltpu.make_async_remote_copy(
            src_ref=src.at[piece], dst_ref=imgs.at[block, piece],
            send_sem=img_send.at[way, lax.div(block, 2), k],
            recv_sem=img_recv.at[block, k], device_id={"tpl": to}, device_id_type=MESH)

    def share_rows(owner, k):
        return pl.ds(owner * quarter + k * t_size, t_size)

    def end_copy(k):
        piece = share_rows(me_i, k)
        return pltpu.make_async_remote_copy(
            src_ref=t_hbm.at[piece], dst_ref=et_ref.at[piece], send_sem=et_send.at[0, k],
            recv_sem=et_recv.at[me_i, k], device_id={"tpl": inner}, device_id_type=MESH)

    def spread_copy(off, k):
        piece = share_rows(me_i, k)
        return pltpu.make_async_remote_copy(
            src_ref=et_ref.at[piece], dst_ref=et_ref.at[piece], send_sem=et_send.at[off, k],
            recv_sem=et_recv.at[me_i, k], device_id={"img": img_peer(off)}, device_id_type=MESH)

    def end_arrival(owner, k):
        piece = share_rows(owner, k)
        return pltpu.make_async_remote_copy(
            src_ref=et_ref.at[piece], dst_ref=et_ref.at[piece], send_sem=et_send.at[0, k],
            recv_sem=et_recv.at[owner, k], device_id={"img": img_peer(1)}, device_id_type=MESH)

    own_block = 2 * chip + core
    sends_out = jnp.logical_and(rank > 0, jnp.logical_not(is_hub))
    if hubs:
        @pl.when(is_end)
        def _():
            for k in range(t_parts):
                end_copy(k).start()

    for k in range(parts):
        if chips > 1:
            image_copy(x_ref, own_block, k, 0, inner).start()

        @pl.when(sends_out)
        def _():
            image_copy(x_ref, own_block, k, 1, outer).start()

        image_copy(x_ref, own_block, k, 2, sibling).start()

    for load in (load_t, load_x, load_mask):
        load.wait()

    def half_norm(ref):
        tf = ref[...].astype(jnp.float32)
        return 0.5 * jnp.sum(tf * tf, axis=1, keepdims=True)

    sqn[...] = half_norm(t_ref)
    acc[...] = jnp.zeros_like(acc)
    occ[...] = jnp.zeros_like(occ)

    def stat_copy(q, slot, off, sems):
        return pltpu.make_async_remote_copy(
            src_ref=st.at[q, slot], dst_ref=st.at[q, slot], send_sem=sems.at[q, off],
            recv_sem=st_recv.at[q, slot], device_id={"tpl": tpl_peer(off)}, device_id_type=MESH)

    def stat_arrival(q, slot):
        return pltpu.make_async_remote_copy(
            src_ref=st.at[q, slot], dst_ref=st.at[q, slot], send_sem=st_send.at[q, 0],
            recv_sem=st_recv.at[q, slot], device_id={"tpl": tpl_peer(1)}, device_id_type=MESH)

    def tell(q, slot, sems):
        for off in range(1, n_tpl):
            @pl.when(jnp.logical_not(absent(q, lax.div(tpl_peer(off), 2))))
            def _():
                stat_copy(q, slot, off, sems).start()

    def told(q, slot, sems):
        for off in range(1, n_tpl):
            @pl.when(jnp.logical_not(absent(q, lax.div(tpl_peer(off), 2))))
            def _():
                stat_copy(q, slot, off, sems).wait_send()

    def pair_of(q):
        return imgs[pl.ds(2 * q, 2)].reshape(2 * rows, feats)

    class_count = power_ref.shape[0]
    per_class = tpl_rows * n_tpl // class_count
    pair = 2 * rows
    for q in range(chips):
        allow[q] = mask_ref[:, q * pair:(q + 1) * pair]

    def inverse_temp(c):
        power = jnp.full((1, pair), power_ref[c], jnp.int32)
        return 0.5 * jnp.exp2(0.5 * power.astype(jnp.float32))

    def class_terms(slot, q):
        first = slot * tpl_rows
        if per_class % tpl_rows == 0:
            only = lax.div(first, per_class)
            return inverse_temp(only), allow[q, pl.ds(only, 1), :] > 0
        owner = lax.div(first + lax.broadcasted_iota(jnp.int32, (tpl_rows, pair), 0), per_class)
        beta = sum(jnp.where(owner == c, inverse_temp(c), 0.0) for c in range(class_count))
        return beta, sum(jnp.where(owner == c, allow[q, c:c + 1, :], 0) for c in range(class_count)) > 0

    def score(q, slot, tpl, norm, e_out):
        raw = lax.dot_general(
            tpl[...], pair_of(q), (((1,), (1,)), ((), ())), preferred_element_type=jnp.float32)
        beta, allowed = class_terms(slot, q)
        s = beta * (raw - norm[...])
        top = jnp.max(jnp.where(allowed, s, floor_score), axis=0, keepdims=True)
        e = jnp.where(allowed, jnp.exp(s - top), 0.0)
        st[q, slot, 0:1, :] = top
        st[q, slot, 1:2, :] = jnp.sum(e, axis=0, keepdims=True)
        e_out[...] = e

    def wait_image(block, k):
        image_copy(imgs.at[block], block, k, 2, sibling).wait_recv()

    def relay(q, k, more, way, to):
        block = 2 * q + core
        wait_image(block, k)

        @pl.when(more)
        def _():
            image_copy(imgs.at[block], block, k, way, to).start()

        image_copy(imgs.at[block], block, k, 2, sibling).start()

    def finish(q):
        for k in range(parts):
            wait_image(2 * q + 1 - core, k)
        score(q, me_t, t_ref, sqn, e_ref.at[q])
        tell(q, me_t, st_send)

    def gather_stats(q):
        for off in range(1, n_tpl):
            slot = tpl_peer(off)

            @pl.when(jnp.logical_not(is_hub & (q == chip) & (slot == end_slot)))
            def _():
                stat_arrival(q, slot).wait_recv()

        tops = [st[q, j, 0:1, :] for j in range(n_tpl)]
        top = functools.reduce(jnp.maximum, tops)
        total = sum(st[q, j, 1:2, :] * jnp.exp(tops[j] - top) for j in range(n_tpl))
        le_row[q] = top + jnp.log(total)
        return top, total

    def weigh(q, slot, e, top, total):
        return e[...] * (jnp.exp(st[q, slot, 0:1, :] - top) / total)

    def consume(q):
        top, total = gather_stats(q)
        post = weigh(q, me_t, e_ref.at[q], top, total)
        occ[...] += jnp.sum(post, axis=1, keepdims=True)
        post_ref[q] = post.astype(jnp.bfloat16)
        return top, total

    bits = [1 << k for k in range(n_img.bit_length() - 1)]
    groups = len(bits) if bits and tpl_rows % (16 * len(bits)) == 0 else 1
    depth = tpl_rows // groups
    orders = [bits[g:] + bits[:g] for g in range(groups)]
    masks = sorted(range(1, n_img), key=lambda mask: -mask.bit_count())

    def flip(mask):
        return me_i + sum(b - 2 * b * lax.rem(lax.div(me_i, b), 2) for b in bits if b & mask)

    def turn(g, mask):
        return next(r for r, b in enumerate(orders[g]) if b & mask)

    def band(g):
        return slice(g * depth, (g + 1) * depth)

    def part_of(mask):
        return pl.ds(pl.multiple_of(flip(mask) * cols, cols), cols)

    class Reduction:
        def __init__(self, src, dst, sent, got, share):
            self.src, self.dst, self.sent, self.got, self.share = src, dst, sent, got, share

        def copy(self, g, mask):
            return pltpu.make_async_remote_copy(
                src_ref=self.src.at[mask, band(g)], dst_ref=self.dst.at[mask, band(g)],
                send_sem=self.sent.at[g, mask], recv_sem=self.got.at[g, mask],
                device_id={"img": flip(orders[g][turn(g, mask)])}, device_id_type=MESH)

        def received(self, g, mask, rounds):
            value = 0.0
            for b in orders[g][:rounds]:
                self.copy(g, b + mask).wait_recv()
                value += self.dst[b + mask, band(g)].astype(jnp.float32)
            return value

        def round(self, r):
            for mask in masks:
                for g in range(groups):
                    if turn(g, mask) == r:
                        value = self.share(g, mask)
                        self.src[mask, band(g)] = (value + self.received(g, mask, r)).astype(jnp.bfloat16)
                        self.copy(g, mask).start()

        def drain(self):
            for mask in masks:
                for g in range(groups):
                    self.copy(g, mask).wait_send()

    def share_end(g, mask):
        block = imgs[pl.ds(2 * chip, 2), :, part_of(mask)].reshape(2 * rows, cols)
        return jnp.dot(post_end[band(g)], block, preferred_element_type=jnp.float32)

    reduce_end = Reduction(sbuf_end, rbuf_end, ers_send, ers_recv, share_end)

    def row_of(column):
        return jnp.transpose(jnp.broadcast_to(column, (tpl_rows, 128)))[0:8]

    def hand_occ():
        return pltpu.make_async_remote_copy(
            src_ref=obuf_end, dst_ref=orecv_end, send_sem=hand_send.at[0],
            recv_sem=hand_recv.at[0], device_id={"tpl": outer}, device_id_type=MESH)

    def hand_evidence(q):
        return pltpu.make_async_remote_copy(
            src_ref=le_row.at[q], dst_ref=le_row.at[q], send_sem=hand_send.at[1],
            recv_sem=hand_recv.at[1], device_id={"tpl": outer}, device_id_type=MESH)

    def hand_sum(g):
        return pltpu.make_async_remote_copy(
            src_ref=zsend.at[band(g)], dst_ref=zrecv.at[band(g)], send_sem=z_send.at[g],
            recv_sem=z_recv.at[g], device_id={"tpl": outer}, device_id_type=MESH)

    def hub_spread(k):
        end_arrival(me_i, k).wait_recv()
        for off in range(1, n_img):
            spread_copy(off, k).start()

    def hub_score():
        for off in range(1, n_img):
            for k in range(t_parts):
                end_arrival(img_peer(off), k).wait_recv()
        sqn_end[...] = half_norm(et_ref)
        score(chip, end_slot, et_ref, sqn_end, e_end)
        tell(chip, end_slot, est_send)

    def hub_consume():
        top, total = consume(chip)
        post = weigh(chip, end_slot, e_end, top, total)
        obuf_end[...] = row_of(jnp.sum(post, axis=1, keepdims=True))
        post_end[...] = post.astype(jnp.bfloat16)
        hand_occ().start()
        hand_evidence(chip).start()

    def hub_reduce():
        reduce_end.round(0)
        for g in range(groups):
            own_end[band(g)] = share_end(g, 0)

    finish(chip)
    n_far = last - rank - skip
    late = parts // 2 if hubs else 0

    def arrive(b, carry):
        q_far = chip + inward * (b + 1 + skip)

        def near_event(block, k):
            q_near = chip - inward * (block + 1)
            there = jnp.logical_and(block >= 0, block < rank)

            @pl.when(there)
            def _():
                relay(q_near, k, last > 0, 0, inner)

            if k == parts - 1:
                @pl.when(there)
                def _():
                    finish(q_near)

        for k in range(parts):
            @pl.when(b < n_far)
            def _():
                relay(q_far, k, rank > 0, 1, outer)

            if k >= late:
                near_event(b, k - late)
            else:
                near_event(b - 1, k - late + parts)
            if hubs:
                spreads = [j for j in range(t_parts) if k == min(j + 1, parts - 1)]
                if spreads:
                    @pl.when(jnp.logical_and(is_hub, b == 0))
                    def _():
                        for j in spreads:
                            hub_spread(j)

                steps = ((parts // 3 - 1, hub_score), (parts // 2, hub_consume), (parts // 2 + 1, hub_reduce))
                due = [step for at, step in steps if k == max(0, min(at, parts - 1))]
                if due:
                    @pl.when(jnp.logical_and(is_hub, b == 1))
                    def _():
                        for step in due:
                            step()

        @pl.when(b < n_far)
        def _():
            finish(q_far)

        return carry

    lax.fori_loop(0, last - 1 if hubs else last, arrive, 0)

    if hubs:
        @pl.when(is_hub)
        def _():
            for r in range(1, len(bits)):
                reduce_end.round(r)

    def middle(q, carry):
        @pl.when(jnp.logical_not(jnp.logical_or(absent(q, chip), is_hub & (q == chip))))
        def _():
            consume(q)

        @pl.when(jnp.logical_not(absent(q, chip)))
        def _():
            for j in range(n_img):
                part = slice(j * cols, (j + 1) * cols)
                block = imgs[pl.ds(2 * q, 2), :, part].reshape(2 * rows, cols)
                acc[:, part] += jnp.dot(post_ref[q], block, preferred_element_type=jnp.float32)

        return carry

    lax.fori_loop(1, chips - 1, middle, 0)

    if hubs:
        @pl.when(is_hub)
        def _():
            for g in range(groups):
                zsend[band(g)] = (own_end[band(g)] + reduce_end.received(g, 0, len(bits))).astype(jnp.bfloat16)
                hand_sum(g).start()

    ends = (0, chips - 1) if chips > 1 else (0,)
    for q in ends:
        consume(q)

    def occ_copy(off):
        return pltpu.make_async_remote_copy(
            src_ref=obuf, dst_ref=orecv.at[off], send_sem=oc_send.at[off],
            recv_sem=oc_recv.at[off], device_id={"img": img_peer(off)}, device_id_type=MESH)

    def share(g, mask):
        part = part_of(mask)
        value = acc[band(g), part]
        for q in ends:
            block = imgs[2 * q:2 * q + 2, :, part].reshape(2 * rows, cols)
            value += jnp.dot(post_ref[q, band(g)], block, preferred_element_type=jnp.float32)
        return value

    reduce_own = Reduction(sbuf, rbuf, rs_send, rs_recv, share)
    obuf[...] = row_of(occ[...])
    if hubs:
        @pl.when(is_end)
        def _():
            hand_occ().wait_recv()
            hand_evidence(chip + inward).wait_recv()
            obuf[...] += orecv_end[...]

    for off in range(1, n_img):
        occ_copy(off).start()
    for q in range(chips):
        le_ref[:, q * pair:(q + 1) * pair] = le_row[q]
    mine = part_of(0)
    for r in range(len(bits)):
        reduce_own.round(r)
        if r == 0:
            for g in range(groups):
                own[band(g)] = share(g, 0) + t_ref[band(g), mine].astype(jnp.float32)
            occ_row = obuf[...]
            for off in range(1, n_img):
                occ_copy(off).wait_recv()
                occ_row += orecv[off]
            occ_col = jnp.transpose(jnp.broadcast_to(occ_row[0:1], (128, tpl_rows)))[:, 0:1]
            occ[...] = occ_col + 1.0
    if hubs:
        @pl.when(is_end)
        def _():
            for g in range(groups):
                hand_sum(g).wait_recv()
                own[band(g)] += zrecv[band(g)].astype(jnp.float32)

    for g in range(groups):
        out_ref[band(g)] = (own[band(g)] + reduce_own.received(g, 0, len(bits))) / occ[band(g)]

    for off in range(1, n_img):
        occ_copy(off).wait_send()
    reduce_own.drain()
    if hubs:
        @pl.when(is_end)
        def _():
            for k in range(t_parts):
                end_copy(k).wait_send()

        @pl.when(is_hub)
        def _():
            for off in range(1, n_img):
                for k in range(t_parts):
                    spread_copy(off, k).wait_send()
            told(chip, end_slot, est_send)
            hand_occ().wait_send()
            hand_evidence(chip).wait_send()
            reduce_end.drain()
            for g in range(groups):
                hand_sum(g).wait_send()

    def drain(q, carry):
        block = 2 * q + core
        away = (q - chip) * inward
        goes_out = (rank > 0) & (away >= 0) & jnp.logical_not(is_hub & (away == 0))
        for k in range(parts):
            @pl.when((away <= 0) & (last > 0))
            def _():
                image_copy(imgs.at[block], block, k, 0, inner).wait_send()

            @pl.when(goes_out)
            def _():
                image_copy(imgs.at[block], block, k, 1, outer).wait_send()

            @pl.when(jnp.logical_not(absent(q, chip)))
            def _():
                image_copy(imgs.at[block], block, k, 2, sibling).wait_send()

        @pl.when(jnp.logical_not(absent(q, chip)))
        def _():
            told(q, me_t, st_send)

        return carry

    lax.fori_loop(0, chips, drain, 0)


def emit(new_ref, evidence_ref, new_out, evidence_out):
    new_out[...] = new_ref[...]
    evidence_out[...] = evidence_ref[...].reshape(evidence_out.shape)


def solution(mesh):
    n_img, n_tpl = mesh.shape["img"], mesh.shape["tpl"]
    chips = n_tpl // 2

    def per_device(images, templates, class_exponent, class_mask):
        rows, feats = images.shape
        tpl_rows = templates.shape[0]
        cols = feats // n_img
        class_count = class_exponent.shape[0]
        parts = max(c for c in (6, 3, 2, 1) if rows % (16 * c) == 0 or c == 1)
        dma = pltpu.SemaphoreType.DMA
        vmem = pl.BlockSpec(memory_space=pltpu.VMEM)
        far = pl.BlockSpec(memory_space=pl.ANY)
        new, evidence = pl.pallas_call(
            functools.partial(kernel, n_img, n_tpl, parts),
            out_shape=(
                jax.ShapeDtypeStruct((tpl_rows, cols), jnp.float32),
                jax.ShapeDtypeStruct((1, n_tpl * rows), jnp.float32),
            ),
            in_specs=[far, far, pl.BlockSpec(memory_space=pltpu.SMEM), far],
            out_specs=(vmem, vmem),
            scratch_shapes=[
                pltpu.VMEM((tpl_rows, feats), jnp.bfloat16),
                pltpu.VMEM((class_count, n_tpl * rows), jnp.int32),
                dma((3,)),
                pltpu.VMEM((n_tpl, rows, feats), jnp.bfloat16),
                pltpu.VMEM((chips, class_count, 2 * rows), jnp.int32),
                pltpu.VMEM((chips, 1, 2 * rows), jnp.float32),
                pltpu.VMEM((chips, tpl_rows, 2 * rows), jnp.float32),
                pltpu.VMEM((chips, tpl_rows, 2 * rows), jnp.bfloat16),
                pltpu.VMEM((chips, n_tpl, 2, 2 * rows), jnp.float32),
                pltpu.VMEM((tpl_rows, feats), jnp.float32),
                pltpu.VMEM((tpl_rows, cols), jnp.float32),
                pltpu.VMEM((n_img, tpl_rows, cols), jnp.bfloat16),
                pltpu.VMEM((n_img, tpl_rows, cols), jnp.bfloat16),
                pltpu.VMEM((tpl_rows, 1), jnp.float32),
                pltpu.VMEM((tpl_rows, 1), jnp.float32),
                pltpu.VMEM((8, tpl_rows), jnp.float32),
                pltpu.VMEM((n_img, 8, tpl_rows), jnp.float32),
                dma((3, chips, parts)),
                dma((n_tpl, parts)),
                dma((chips, n_tpl)),
                dma((chips, n_tpl)),
                dma((n_img, n_img)),
                dma((n_img, n_img)),
                dma((n_img,)),
                dma((n_img,)),
                pltpu.VMEM((tpl_rows, feats), jnp.bfloat16),
                pltpu.VMEM((tpl_rows, 2 * rows), jnp.float32),
                pltpu.VMEM((tpl_rows, 2 * rows), jnp.bfloat16),
                pltpu.VMEM((tpl_rows, 1), jnp.float32),
                pltpu.VMEM((tpl_rows, 1), jnp.float32),
                pltpu.VMEM((tpl_rows, cols), jnp.float32),
                pltpu.VMEM((n_img, tpl_rows, cols), jnp.bfloat16),
                pltpu.VMEM((n_img, tpl_rows, cols), jnp.bfloat16),
                pltpu.VMEM((tpl_rows, cols), jnp.bfloat16),
                pltpu.VMEM((tpl_rows, cols), jnp.bfloat16),
                pltpu.VMEM((8, tpl_rows), jnp.float32),
                pltpu.VMEM((8, tpl_rows), jnp.float32),
                dma((n_img, 2)),
                dma((n_img, 2)),
                dma((chips, n_tpl)),
                dma((n_img, n_img)),
                dma((n_img, n_img)),
                dma((n_img,)),
                dma((n_img,)),
                dma((2,)),
                dma((2,)),
            ],
            compiler_params=pltpu.CompilerParams(
                collective_id=0, has_side_effects=True, vmem_limit_bytes=60 * 1024 * 1024),
        )(images, templates, class_exponent, class_mask.T)
        return pl.pallas_call(
            emit,
            out_shape=(
                jax.ShapeDtypeStruct(new.shape, jnp.float32),
                jax.ShapeDtypeStruct((n_tpl * rows,), jnp.float32),
            ),
            in_specs=[vmem] * 2,
            out_specs=(vmem, vmem),
        )(new, evidence)

    in_specs = (P(("img", "tpl"), None), P("tpl", None), P(), P("img", None))
    out_specs = (P("tpl", "img"), P("img"))
    return jax.shard_map(
        per_device, mesh=mesh, in_specs=in_specs, out_specs=out_specs, check_vma=False
    )
```

```python
import functools

import jax
import jax.numpy as jnp
from jax import lax
from jax.experimental import pallas as pl
from jax.experimental.pallas import tpu as pltpu
from jax.sharding import PartitionSpec as P

MESH = pl.DeviceIdType.MESH
floor_score = -1e30


def kernel(
    n_img, n_tpl, parts, x_ref, t_hbm, power_ref, mask_hbm, out_ref, le_ref,
    t_ref, mask_ref, loads, imgs, allow, le_row, e_ref, post_ref, st, acc, own, sbuf, rbuf, sqn, occ, obuf, orecv,
    img_send, img_recv, st_send, st_recv, rs_send, rs_recv, oc_send, oc_recv,
    et_ref, e_end, post_end, sqn_end, occ_end, own_end, sbuf_end, rbuf_end, zsend, zrecv, obuf_end, orecv_end,
    et_send, et_recv, est_send, ers_send, ers_recv, z_send, z_recv, hand_send, hand_recv,
):
    chips = n_tpl // 2
    last = chips - 1
    hubs = chips >= 4
    rows, feats = x_ref.shape
    cols = feats // n_img
    me_i, me_t = lax.axis_index("img"), lax.axis_index("tpl")
    chip, core = lax.div(me_t, 2), lax.rem(me_t, 2)
    sibling = 2 * chip + 1 - core
    side = lax.div(2 * chip, chips)
    inward = 1 - 2 * side
    rank = chip + side * (last - 2 * chip)
    inner, outer = me_t + 2 * inward, me_t - 2 * inward
    is_end = jnp.logical_and(rank == 0, hubs)
    is_hub = jnp.logical_and(rank == 1, hubs)
    skip = jnp.where(is_end, 1, 0)
    end_slot = outer

    def absent(q, who):
        if not hubs:
            return False
        low = jnp.logical_and(q == 1, who == 0)
        return jnp.logical_or(low, jnp.logical_and(q == last - 1, who == last))

    def tpl_peer(off):
        return lax.rem(me_t + off, n_tpl)

    def img_peer(off):
        return lax.rem(me_i + off, n_img)

    barrier = pltpu.get_barrier_semaphore()
    for off in range(1, n_tpl):
        pl.semaphore_signal(barrier, inc=1, device_id={"tpl": tpl_peer(off)}, device_id_type=MESH)
    for off in range(1, n_img):
        pl.semaphore_signal(barrier, inc=1, device_id={"img": img_peer(off)}, device_id_type=MESH)
    load_t = pltpu.make_async_copy(t_hbm, t_ref, loads.at[0])
    load_x = pltpu.make_async_copy(x_ref, imgs.at[me_t], loads.at[1])
    load_mask = pltpu.make_async_copy(mask_hbm, mask_ref, loads.at[2])
    for load in (load_t, load_x, load_mask):
        load.start()
    pl.semaphore_wait(barrier, n_tpl - 1 + n_img - 1)

    size = rows // parts
    tpl_rows = t_ref.shape[0]
    quarter = tpl_rows // n_img
    t_parts = 2 if quarter % 32 == 0 else 1
    t_size = quarter // t_parts

    def image_copy(src, block, k, way, to):
        piece = pl.ds(k * size, size)
        return pltpu.make_async_remote_copy(
            src_ref=src.at[piece], dst_ref=imgs.at[block, piece],
            send_sem=img_send.at[way, lax.div(block, 2), k],
            recv_sem=img_recv.at[block, k], device_id={"tpl": to}, device_id_type=MESH)

    def share_rows(owner, k):
        return pl.ds(owner * quarter + k * t_size, t_size)

    def end_copy(k):
        piece = share_rows(me_i, k)
        return pltpu.make_async_remote_copy(
            src_ref=t_hbm.at[piece], dst_ref=et_ref.at[piece], send_sem=et_send.at[0, k],
            recv_sem=et_recv.at[me_i, k], device_id={"tpl": inner}, device_id_type=MESH)

    def spread_copy(off, k):
        piece = share_rows(me_i, k)
        return pltpu.make_async_remote_copy(
            src_ref=et_ref.at[piece], dst_ref=et_ref.at[piece], send_sem=et_send.at[off, k],
            recv_sem=et_recv.at[me_i, k], device_id={"img": img_peer(off)}, device_id_type=MESH)

    def end_arrival(owner, k):
        piece = share_rows(owner, k)
        return pltpu.make_async_remote_copy(
            src_ref=et_ref.at[piece], dst_ref=et_ref.at[piece], send_sem=et_send.at[0, k],
            recv_sem=et_recv.at[owner, k], device_id={"img": img_peer(1)}, device_id_type=MESH)

    own_block = 2 * chip + core
    sends_out = jnp.logical_and(rank > 0, jnp.logical_not(is_hub))
    if hubs:
        @pl.when(is_end)
        def _():
            for k in range(t_parts):
                end_copy(k).start()

    for k in range(parts):
        if chips > 1:
            image_copy(x_ref, own_block, k, 0, inner).start()

        @pl.when(sends_out)
        def _():
            image_copy(x_ref, own_block, k, 1, outer).start()

        image_copy(x_ref, own_block, k, 2, sibling).start()

    for load in (load_t, load_x, load_mask):
        load.wait()

    def half_norm(ref):
        tf = ref[...].astype(jnp.float32)
        return 0.5 * jnp.sum(tf * tf, axis=1, keepdims=True)

    sqn[...] = half_norm(t_ref)
    acc[...] = jnp.zeros_like(acc)
    occ[...] = jnp.zeros_like(occ)

    def stat_copy(q, slot, off, sems):
        return pltpu.make_async_remote_copy(
            src_ref=st.at[q, slot], dst_ref=st.at[q, slot], send_sem=sems.at[q, off],
            recv_sem=st_recv.at[q, slot], device_id={"tpl": tpl_peer(off)}, device_id_type=MESH)

    def stat_arrival(q, slot):
        return pltpu.make_async_remote_copy(
            src_ref=st.at[q, slot], dst_ref=st.at[q, slot], send_sem=st_send.at[q, 0],
            recv_sem=st_recv.at[q, slot], device_id={"tpl": tpl_peer(1)}, device_id_type=MESH)

    def tell(q, slot, sems):
        for off in range(1, n_tpl):
            @pl.when(jnp.logical_not(absent(q, lax.div(tpl_peer(off), 2))))
            def _():
                stat_copy(q, slot, off, sems).start()

    def told(q, slot, sems):
        for off in range(1, n_tpl):
            @pl.when(jnp.logical_not(absent(q, lax.div(tpl_peer(off), 2))))
            def _():
                stat_copy(q, slot, off, sems).wait_send()

    def pair_of(q):
        return imgs[pl.ds(2 * q, 2)].reshape(2 * rows, feats)

    class_count = power_ref.shape[0]
    per_class = tpl_rows * n_tpl // class_count
    pair = 2 * rows
    for q in range(chips):
        allow[q] = mask_ref[:, q * pair:(q + 1) * pair]

    def inverse_temp(c):
        power = jnp.full((1, pair), power_ref[c], jnp.int32)
        return 0.5 * jnp.exp2(0.5 * power.astype(jnp.float32))

    def class_terms(slot, q):
        first = slot * tpl_rows
        if per_class % tpl_rows == 0:
            only = lax.div(first, per_class)
            return inverse_temp(only), allow[q, pl.ds(only, 1), :] > 0
        owner = lax.div(first + lax.broadcasted_iota(jnp.int32, (tpl_rows, pair), 0), per_class)
        beta = sum(jnp.where(owner == c, inverse_temp(c), 0.0) for c in range(class_count))
        return beta, sum(jnp.where(owner == c, allow[q, c:c + 1, :], 0) for c in range(class_count)) > 0

    def score(q, slot, tpl, norm, e_out):
        raw = lax.dot_general(
            tpl[...], pair_of(q), (((1,), (1,)), ((), ())), preferred_element_type=jnp.float32)
        beta, allowed = class_terms(slot, q)
        s = beta * (raw - norm[...])
        top = jnp.max(jnp.where(allowed, s, floor_score), axis=0, keepdims=True)
        e = jnp.where(allowed, jnp.exp(s - top), 0.0)
        st[q, slot, 0:1, :] = top
        st[q, slot, 1:2, :] = jnp.sum(e, axis=0, keepdims=True)
        e_out[...] = e

    def wait_image(block, k):
        image_copy(imgs.at[block], block, k, 2, sibling).wait_recv()

    def relay(q, k, more, way, to):
        block = 2 * q + core
        wait_image(block, k)

        @pl.when(more)
        def _():
            image_copy(imgs.at[block], block, k, way, to).start()

        image_copy(imgs.at[block], block, k, 2, sibling).start()

    def finish(q):
        for k in range(parts):
            wait_image(2 * q + 1 - core, k)
        score(q, me_t, t_ref, sqn, e_ref.at[q])
        tell(q, me_t, st_send)

    def gather_stats(q):
        for off in range(1, n_tpl):
            slot = tpl_peer(off)

            @pl.when(jnp.logical_not(is_hub & (q == chip) & (slot == end_slot)))
            def _():
                stat_arrival(q, slot).wait_recv()

        tops = [st[q, j, 0:1, :] for j in range(n_tpl)]
        top = functools.reduce(jnp.maximum, tops)
        total = sum(st[q, j, 1:2, :] * jnp.exp(tops[j] - top) for j in range(n_tpl))
        le_row[q] = top + jnp.log(total)
        return top, total

    def weigh(q, slot, e, top, total):
        return e[...] * (jnp.exp(st[q, slot, 0:1, :] - top) / total)

    def consume(q):
        top, total = gather_stats(q)
        post = weigh(q, me_t, e_ref.at[q], top, total)
        occ[...] += jnp.sum(post, axis=1, keepdims=True)
        post_ref[q] = post.astype(jnp.bfloat16)
        return top, total

    bits = [1 << k for k in range(n_img.bit_length() - 1)]
    groups = len(bits) if bits and tpl_rows % (16 * len(bits)) == 0 else 1
    depth = tpl_rows // groups
    orders = [bits[g:] + bits[:g] for g in range(groups)]
    masks = sorted(range(1, n_img), key=lambda mask: -mask.bit_count())

    def flip(mask):
        return me_i + sum(b - 2 * b * lax.rem(lax.div(me_i, b), 2) for b in bits if b & mask)

    def turn(g, mask):
        return next(r for r, b in enumerate(orders[g]) if b & mask)

    def band(g):
        return slice(g * depth, (g + 1) * depth)

    def part_of(mask):
        return pl.ds(pl.multiple_of(flip(mask) * cols, cols), cols)

    class Reduction:
        def __init__(self, src, dst, sent, got, share):
            self.src, self.dst, self.sent, self.got, self.share = src, dst, sent, got, share

        def copy(self, g, mask):
            return pltpu.make_async_remote_copy(
                src_ref=self.src.at[mask, band(g)], dst_ref=self.dst.at[mask, band(g)],
                send_sem=self.sent.at[g, mask], recv_sem=self.got.at[g, mask],
                device_id={"img": flip(orders[g][turn(g, mask)])}, device_id_type=MESH)

        def received(self, g, mask, rounds):
            value = 0.0
            for b in orders[g][:rounds]:
                self.copy(g, b + mask).wait_recv()
                value += self.dst[b + mask, band(g)].astype(jnp.float32)
            return value

        def round(self, r):
            for mask in masks:
                for g in range(groups):
                    if turn(g, mask) == r:
                        value = self.share(g, mask)
                        self.src[mask, band(g)] = (value + self.received(g, mask, r)).astype(jnp.bfloat16)
                        self.copy(g, mask).start()

        def drain(self):
            for mask in masks:
                for g in range(groups):
                    self.copy(g, mask).wait_send()

    def share_end(g, mask):
        block = imgs[pl.ds(2 * chip, 2), :, part_of(mask)].reshape(2 * rows, cols)
        return jnp.dot(post_end[band(g)], block, preferred_element_type=jnp.float32)

    reduce_end = Reduction(sbuf_end, rbuf_end, ers_send, ers_recv, share_end)

    def row_of(column):
        return jnp.transpose(jnp.broadcast_to(column, (tpl_rows, 128)))[0:8]

    def hand_occ():
        return pltpu.make_async_remote_copy(
            src_ref=obuf_end, dst_ref=orecv_end, send_sem=hand_send.at[0],
            recv_sem=hand_recv.at[0], device_id={"tpl": outer}, device_id_type=MESH)

    def hand_evidence(q):
        return pltpu.make_async_remote_copy(
            src_ref=le_row.at[q], dst_ref=le_row.at[q], send_sem=hand_send.at[1],
            recv_sem=hand_recv.at[1], device_id={"tpl": outer}, device_id_type=MESH)

    def hand_sum(g):
        return pltpu.make_async_remote_copy(
            src_ref=zsend.at[band(g)], dst_ref=zrecv.at[band(g)], send_sem=z_send.at[g],
            recv_sem=z_recv.at[g], device_id={"tpl": outer}, device_id_type=MESH)

    def hub_spread(k):
        end_arrival(me_i, k).wait_recv()
        for off in range(1, n_img):
            spread_copy(off, k).start()

    def hub_score():
        for off in range(1, n_img):
            for k in range(t_parts):
                end_arrival(img_peer(off), k).wait_recv()
        sqn_end[...] = half_norm(et_ref)
        score(chip, end_slot, et_ref, sqn_end, e_end)
        tell(chip, end_slot, est_send)

    def hub_consume():
        top, total = consume(chip)
        post = weigh(chip, end_slot, e_end, top, total)
        obuf_end[...] = row_of(jnp.sum(post, axis=1, keepdims=True))
        post_end[...] = post.astype(jnp.bfloat16)
        hand_occ().start()
        hand_evidence(chip).start()

    def hub_reduce():
        reduce_end.round(0)
        for g in range(groups):
            own_end[band(g)] = share_end(g, 0)

    finish(chip)
    n_far = last - rank - skip
    late = parts // 2 if hubs else 0

    def arrive(b, carry):
        q_far = chip + inward * (b + 1 + skip)

        def near_event(block, k):
            q_near = chip - inward * (block + 1)
            there = jnp.logical_and(block >= 0, block < rank)

            @pl.when(there)
            def _():
                relay(q_near, k, last > 0, 0, inner)

            if k == parts - 1:
                @pl.when(there)
                def _():
                    finish(q_near)

        for k in range(parts):
            @pl.when(b < n_far)
            def _():
                relay(q_far, k, rank > 0, 1, outer)

            if k >= late:
                near_event(b, k - late)
            else:
                near_event(b - 1, k - late + parts)
            if hubs:
                spreads = [j for j in range(t_parts) if k == min(j + 1, parts - 1)]
                if spreads:
                    @pl.when(jnp.logical_and(is_hub, b == 0))
                    def _():
                        for j in spreads:
                            hub_spread(j)

                steps = ((parts // 3 - 1, hub_score), (parts // 2, hub_consume), (parts // 2 + 1, hub_reduce))
                due = [step for at, step in steps if k == max(0, min(at, parts - 1))]
                if due:
                    @pl.when(jnp.logical_and(is_hub, b == 1))
                    def _():
                        for step in due:
                            step()

        @pl.when(b < n_far)
        def _():
            finish(q_far)

        return carry

    lax.fori_loop(0, last - 1 if hubs else last, arrive, 0)

    if hubs:
        @pl.when(is_hub)
        def _():
            for r in range(1, len(bits)):
                reduce_end.round(r)

    def middle(q, carry):
        @pl.when(jnp.logical_not(jnp.logical_or(absent(q, chip), is_hub & (q == chip))))
        def _():
            consume(q)

        @pl.when(jnp.logical_not(absent(q, chip)))
        def _():
            for j in range(n_img):
                part = slice(j * cols, (j + 1) * cols)
                block = imgs[pl.ds(2 * q, 2), :, part].reshape(2 * rows, cols)
                acc[:, part] += jnp.dot(post_ref[q], block, preferred_element_type=jnp.float32)

        return carry

    lax.fori_loop(1, chips - 1, middle, 0)

    if hubs:
        @pl.when(is_hub)
        def _():
            for g in range(groups):
                zsend[band(g)] = (own_end[band(g)] + reduce_end.received(g, 0, len(bits))).astype(jnp.bfloat16)
                hand_sum(g).start()

    ends = (0, chips - 1) if chips > 1 else (0,)
    for q in ends:
        consume(q)

    def occ_copy(off):
        return pltpu.make_async_remote_copy(
            src_ref=obuf, dst_ref=orecv.at[off], send_sem=oc_send.at[off],
            recv_sem=oc_recv.at[off], device_id={"img": img_peer(off)}, device_id_type=MESH)

    def share(g, mask):
        part = part_of(mask)
        value = acc[band(g), part]
        for q in ends:
            block = imgs[2 * q:2 * q + 2, :, part].reshape(2 * rows, cols)
            value += jnp.dot(post_ref[q, band(g)], block, preferred_element_type=jnp.float32)
        return value

    reduce_own = Reduction(sbuf, rbuf, rs_send, rs_recv, share)
    obuf[...] = row_of(occ[...])
    if hubs:
        @pl.when(is_end)
        def _():
            hand_occ().wait_recv()
            hand_evidence(chip + inward).wait_recv()
            obuf[...] += orecv_end[...]

    for off in range(1, n_img):
        occ_copy(off).start()
    for q in range(chips):
        le_ref[:, q * pair:(q + 1) * pair] = le_row[q]
    mine = part_of(0)
    for r in range(len(bits)):
        reduce_own.round(r)
        if r == 0:
            for g in range(groups):
                own[band(g)] = share(g, 0) + t_ref[band(g), mine].astype(jnp.float32)
            occ_row = obuf[...]
            for off in range(1, n_img):
                occ_copy(off).wait_recv()
                occ_row += orecv[off]
            occ_col = jnp.transpose(jnp.broadcast_to(occ_row[0:1], (128, tpl_rows)))[:, 0:1]
            occ[...] = occ_col + 1.0
    if hubs:
        @pl.when(is_end)
        def _():
            for g in range(groups):
                hand_sum(g).wait_recv()
                own[band(g)] += zrecv[band(g)].astype(jnp.float32)

    for g in range(groups):
        out_ref[band(g)] = (own[band(g)] + reduce_own.received(g, 0, len(bits))) / occ[band(g)]

    for off in range(1, n_img):
        occ_copy(off).wait_send()
    reduce_own.drain()
    if hubs:
        @pl.when(is_end)
        def _():
            for k in range(t_parts):
                end_copy(k).wait_send()

        @pl.when(is_hub)
        def _():
            for off in range(1, n_img):
                for k in range(t_parts):
                    spread_copy(off, k).wait_send()
            told(chip, end_slot, est_send)
            hand_occ().wait_send()
            hand_evidence(chip).wait_send()
            reduce_end.drain()
            for g in range(groups):
                hand_sum(g).wait_send()

    def drain(q, carry):
        block = 2 * q + core
        away = (q - chip) * inward
        goes_out = (rank > 0) & (away >= 0) & jnp.logical_not(is_hub & (away == 0))
        for k in range(parts):
            @pl.when((away <= 0) & (last > 0))
            def _():
                image_copy(imgs.at[block], block, k, 0, inner).wait_send()

            @pl.when(goes_out)
            def _():
                image_copy(imgs.at[block], block, k, 1, outer).wait_send()

            @pl.when(jnp.logical_not(absent(q, chip)))
            def _():
                image_copy(imgs.at[block], block, k, 2, sibling).wait_send()

        @pl.when(jnp.logical_not(absent(q, chip)))
        def _():
            told(q, me_t, st_send)

        return carry

    lax.fori_loop(0, chips, drain, 0)


def emit(new_ref, evidence_ref, new_out, evidence_out, sem):
    move = pltpu.make_async_copy(new_ref, new_out, sem)
    move.start()
    evidence_out[...] = evidence_ref[...].reshape(evidence_out.shape)
    move.wait()


def solution(mesh):
    n_img, n_tpl = mesh.shape["img"], mesh.shape["tpl"]
    chips = n_tpl // 2

    def per_device(images, templates, class_exponent, class_mask):
        rows, feats = images.shape
        tpl_rows = templates.shape[0]
        cols = feats // n_img
        class_count = class_exponent.shape[0]
        parts = max(c for c in (6, 3, 2, 1) if rows % (16 * c) == 0 or c == 1)
        dma = pltpu.SemaphoreType.DMA
        vmem = pl.BlockSpec(memory_space=pltpu.VMEM)
        far = pl.BlockSpec(memory_space=pl.ANY)
        new, evidence = pl.pallas_call(
            functools.partial(kernel, n_img, n_tpl, parts),
            out_shape=(
                pltpu.VMEM((tpl_rows, cols), jnp.float32),
                pltpu.VMEM((1, n_tpl * rows), jnp.float32),
            ),
            in_specs=[far, far, pl.BlockSpec(memory_space=pltpu.SMEM), far],
            out_specs=(vmem, vmem),
            scratch_shapes=[
                pltpu.VMEM((tpl_rows, feats), jnp.bfloat16),
                pltpu.VMEM((class_count, n_tpl * rows), jnp.int32),
                dma((3,)),
                pltpu.VMEM((n_tpl, rows, feats), jnp.bfloat16),
                pltpu.VMEM((chips, class_count, 2 * rows), jnp.int32),
                pltpu.VMEM((chips, 1, 2 * rows), jnp.float32),
                pltpu.VMEM((chips, tpl_rows, 2 * rows), jnp.float32),
                pltpu.VMEM((chips, tpl_rows, 2 * rows), jnp.bfloat16),
                pltpu.VMEM((chips, n_tpl, 2, 2 * rows), jnp.float32),
                pltpu.VMEM((tpl_rows, feats), jnp.float32),
                pltpu.VMEM((tpl_rows, cols), jnp.float32),
                pltpu.VMEM((n_img, tpl_rows, cols), jnp.bfloat16),
                pltpu.VMEM((n_img, tpl_rows, cols), jnp.bfloat16),
                pltpu.VMEM((tpl_rows, 1), jnp.float32),
                pltpu.VMEM((tpl_rows, 1), jnp.float32),
                pltpu.VMEM((8, tpl_rows), jnp.float32),
                pltpu.VMEM((n_img, 8, tpl_rows), jnp.float32),
                dma((3, chips, parts)),
                dma((n_tpl, parts)),
                dma((chips, n_tpl)),
                dma((chips, n_tpl)),
                dma((n_img, n_img)),
                dma((n_img, n_img)),
                dma((n_img,)),
                dma((n_img,)),
                pltpu.VMEM((tpl_rows, feats), jnp.bfloat16),
                pltpu.VMEM((tpl_rows, 2 * rows), jnp.float32),
                pltpu.VMEM((tpl_rows, 2 * rows), jnp.bfloat16),
                pltpu.VMEM((tpl_rows, 1), jnp.float32),
                pltpu.VMEM((tpl_rows, 1), jnp.float32),
                pltpu.VMEM((tpl_rows, cols), jnp.float32),
                pltpu.VMEM((n_img, tpl_rows, cols), jnp.bfloat16),
                pltpu.VMEM((n_img, tpl_rows, cols), jnp.bfloat16),
                pltpu.VMEM((tpl_rows, cols), jnp.bfloat16),
                pltpu.VMEM((tpl_rows, cols), jnp.bfloat16),
                pltpu.VMEM((8, tpl_rows), jnp.float32),
                pltpu.VMEM((8, tpl_rows), jnp.float32),
                dma((n_img, 2)),
                dma((n_img, 2)),
                dma((chips, n_tpl)),
                dma((n_img, n_img)),
                dma((n_img, n_img)),
                dma((n_img,)),
                dma((n_img,)),
                dma((2,)),
                dma((2,)),
            ],
            compiler_params=pltpu.CompilerParams(
                collective_id=0, has_side_effects=True, vmem_limit_bytes=60 * 1024 * 1024),
        )(images, templates, class_exponent, class_mask.T)
        return pl.pallas_call(
            emit,
            out_shape=(
                jax.ShapeDtypeStruct(new.shape, jnp.float32),
                jax.ShapeDtypeStruct((n_tpl * rows,), jnp.float32),
            ),
            in_specs=[vmem] * 2,
            out_specs=(far, vmem),
            scratch_shapes=[dma],
        )(*[pltpu.with_memory_space_constraint(x, pltpu.VMEM) for x in (new, evidence)])

    in_specs = (P(("img", "tpl"), None), P("tpl", None), P(), P("img", None))
    out_specs = (P("tpl", "img"), P("img"))
    return jax.shard_map(
        per_device, mesh=mesh, in_specs=in_specs, out_specs=out_specs, check_vma=False
    )
```

```python
import functools

import jax
import jax.numpy as jnp
from jax import lax
from jax.experimental import pallas as pl
from jax.experimental.pallas import tpu as pltpu
from jax.sharding import PartitionSpec as P

MESH = pl.DeviceIdType.MESH
floor_score = -1e30


def kernel(
    n_img, n_tpl, parts, x_ref, t_hbm, power_ref, mask_hbm, out_ref, le_ref,
    t_ref, mask_ref, loads, imgs, allow, le_row, e_ref, post_ref, st, acc, own, sbuf, rbuf, sqn, occ, obuf, orecv,
    img_send, img_recv, st_send, st_recv, rs_send, rs_recv, oc_send, oc_recv,
    et_ref, e_end, post_end, sqn_end, occ_end, own_end, sbuf_end, rbuf_end, zsend, zrecv, obuf_end, orecv_end,
    et_send, et_recv, est_send, ers_send, ers_recv, z_send, z_recv, hand_send, hand_recv,
):
    chips = n_tpl // 2
    last = chips - 1
    hubs = chips >= 4
    rows, feats = x_ref.shape
    cols = feats // n_img
    me_i, me_t = lax.axis_index("img"), lax.axis_index("tpl")
    chip, core = lax.div(me_t, 2), lax.rem(me_t, 2)
    sibling = 2 * chip + 1 - core
    side = lax.div(2 * chip, chips)
    inward = 1 - 2 * side
    rank = chip + side * (last - 2 * chip)
    inner, outer = me_t + 2 * inward, me_t - 2 * inward
    is_end = jnp.logical_and(rank == 0, hubs)
    is_hub = jnp.logical_and(rank == 1, hubs)
    skip = jnp.where(is_end, 1, 0)
    end_slot = outer
    opposite = last * (1 - side)

    def absent(q, who):
        if not hubs:
            return False
        low = jnp.logical_and(q == 1, who == 0)
        return jnp.logical_or(low, jnp.logical_and(q == last - 1, who == last))

    def tpl_peer(off):
        return lax.rem(me_t + off, n_tpl)

    def img_peer(off):
        return lax.rem(me_i + off, n_img)

    barrier = pltpu.get_barrier_semaphore()
    for off in range(1, n_tpl):
        pl.semaphore_signal(barrier, inc=1, device_id={"tpl": tpl_peer(off)}, device_id_type=MESH)
    for off in range(1, n_img):
        pl.semaphore_signal(barrier, inc=1, device_id={"img": img_peer(off)}, device_id_type=MESH)
    load_t = pltpu.make_async_copy(t_hbm, t_ref, loads.at[0])
    load_x = pltpu.make_async_copy(x_ref, imgs.at[me_t], loads.at[1])
    load_mask = pltpu.make_async_copy(mask_hbm, mask_ref, loads.at[2])
    for load in (load_t, load_x, load_mask):
        load.start()
    pl.semaphore_wait(barrier, n_tpl - 1 + n_img - 1)

    size = rows // parts
    tpl_rows = t_ref.shape[0]
    quarter = tpl_rows // n_img
    t_parts = 2 if quarter % 32 == 0 else 1
    t_size = quarter // t_parts

    def image_copy(src, block, k, way, to):
        piece = pl.ds(k * size, size)
        return pltpu.make_async_remote_copy(
            src_ref=src.at[piece], dst_ref=imgs.at[block, piece],
            send_sem=img_send.at[way, lax.div(block, 2), k],
            recv_sem=img_recv.at[block, k], device_id={"tpl": to}, device_id_type=MESH)

    def share_rows(owner, k):
        return pl.ds(owner * quarter + k * t_size, t_size)

    def end_copy(k):
        piece = share_rows(me_i, k)
        return pltpu.make_async_remote_copy(
            src_ref=t_hbm.at[piece], dst_ref=et_ref.at[piece], send_sem=et_send.at[0, k],
            recv_sem=et_recv.at[me_i, k], device_id={"tpl": inner}, device_id_type=MESH)

    def spread_copy(off, k):
        piece = share_rows(me_i, k)
        return pltpu.make_async_remote_copy(
            src_ref=et_ref.at[piece], dst_ref=et_ref.at[piece], send_sem=et_send.at[off, k],
            recv_sem=et_recv.at[me_i, k], device_id={"img": img_peer(off)}, device_id_type=MESH)

    def end_arrival(owner, k):
        piece = share_rows(owner, k)
        return pltpu.make_async_remote_copy(
            src_ref=et_ref.at[piece], dst_ref=et_ref.at[piece], send_sem=et_send.at[0, k],
            recv_sem=et_recv.at[owner, k], device_id={"img": img_peer(1)}, device_id_type=MESH)

    own_block = 2 * chip + core
    sends_out = jnp.logical_and(rank > 0, jnp.logical_not(is_hub))
    if hubs:
        @pl.when(is_end)
        def _():
            for k in range(t_parts):
                end_copy(k).start()

    for k in range(parts):
        if chips > 1:
            image_copy(x_ref, own_block, k, 0, inner).start()

        @pl.when(sends_out)
        def _():
            image_copy(x_ref, own_block, k, 1, outer).start()

        image_copy(x_ref, own_block, k, 2, sibling).start()

    for load in (load_t, load_x, load_mask):
        load.wait()

    def half_norm(ref):
        tf = ref[...].astype(jnp.float32)
        return 0.5 * jnp.sum(tf * tf, axis=1, keepdims=True)

    sqn[...] = half_norm(t_ref)
    acc[...] = jnp.zeros_like(acc)
    occ[...] = jnp.zeros_like(occ)

    def stat_copy(q, slot, off, sems):
        return pltpu.make_async_remote_copy(
            src_ref=st.at[q, slot], dst_ref=st.at[q, slot], send_sem=sems.at[q, off],
            recv_sem=st_recv.at[q, slot], device_id={"tpl": tpl_peer(off)}, device_id_type=MESH)

    def stat_arrival(q, slot):
        return pltpu.make_async_remote_copy(
            src_ref=st.at[q, slot], dst_ref=st.at[q, slot], send_sem=st_send.at[q, 0],
            recv_sem=st_recv.at[q, slot], device_id={"tpl": tpl_peer(1)}, device_id_type=MESH)

    def tell(q, slot, sems):
        for off in range(1, n_tpl):
            @pl.when(jnp.logical_not(absent(q, lax.div(tpl_peer(off), 2))))
            def _():
                stat_copy(q, slot, off, sems).start()

    def told(q, slot, sems):
        for off in range(1, n_tpl):
            @pl.when(jnp.logical_not(absent(q, lax.div(tpl_peer(off), 2))))
            def _():
                stat_copy(q, slot, off, sems).wait_send()

    def pair_of(q):
        return imgs[pl.ds(2 * q, 2)].reshape(2 * rows, feats)

    class_count = power_ref.shape[0]
    per_class = tpl_rows * n_tpl // class_count
    pair = 2 * rows
    for q in range(chips):
        allow[q] = mask_ref[:, q * pair:(q + 1) * pair]

    def inverse_temp(c):
        power = jnp.full((1, pair), power_ref[c], jnp.int32)
        return 0.5 * jnp.exp2(0.5 * power.astype(jnp.float32))

    def class_terms(slot, q):
        first = slot * tpl_rows
        if per_class % tpl_rows == 0:
            only = lax.div(first, per_class)
            return inverse_temp(only), allow[q, pl.ds(only, 1), :] > 0
        owner = lax.div(first + lax.broadcasted_iota(jnp.int32, (tpl_rows, pair), 0), per_class)
        beta = sum(jnp.where(owner == c, inverse_temp(c), 0.0) for c in range(class_count))
        return beta, sum(jnp.where(owner == c, allow[q, c:c + 1, :], 0) for c in range(class_count)) > 0

    def score(q, slot, tpl, norm, e_out):
        raw = lax.dot_general(
            tpl[...], pair_of(q), (((1,), (1,)), ((), ())), preferred_element_type=jnp.float32)
        beta, allowed = class_terms(slot, q)
        s = beta * (raw - norm[...])
        top = jnp.max(jnp.where(allowed, s, floor_score), axis=0, keepdims=True)
        e = jnp.where(allowed, jnp.exp(s - top), 0.0)
        st[q, slot, 0:1, :] = top
        st[q, slot, 1:2, :] = jnp.sum(e, axis=0, keepdims=True)
        if e_out is not None:
            e_out[...] = e

    def wait_image(block, k):
        image_copy(imgs.at[block], block, k, 2, sibling).wait_recv()

    def relay(q, k, more, way, to):
        block = 2 * q + core
        wait_image(block, k)

        @pl.when(more)
        def _():
            image_copy(imgs.at[block], block, k, way, to).start()

        image_copy(imgs.at[block], block, k, 2, sibling).start()

    def finish(q):
        for k in range(parts):
            wait_image(2 * q + 1 - core, k)
        score(q, me_t, t_ref, sqn, e_ref.at[q])
        tell(q, me_t, st_send)

    def finish_given(q):
        for k in range(parts):
            wait_image(2 * q + 1 - core, k)
        raw = lax.dot_general(
            t_ref[...], pair_of(q), (((1,), (1,)), ((), ())), preferred_element_type=jnp.float32)
        beta, allowed = class_terms(me_t, q)
        stat_arrival(q, me_t).wait_recv()
        s = beta * (raw - sqn[...])
        e_ref[q] = jnp.where(allowed, jnp.exp(s - st[q, me_t, 0:1, :]), 0.0)

    def gather_stats(q):
        for off in range(1, n_tpl):
            slot = tpl_peer(off)

            @pl.when(jnp.logical_not(is_hub & ((q == chip) | (q == opposite)) & (slot == end_slot)))
            def _():
                stat_arrival(q, slot).wait_recv()

        tops = [st[q, j, 0:1, :] for j in range(n_tpl)]
        top = functools.reduce(jnp.maximum, tops)
        total = sum(st[q, j, 1:2, :] * jnp.exp(tops[j] - top) for j in range(n_tpl))
        le_row[q] = top + jnp.log(total)
        return top, total

    def weigh(q, slot, e, top, total):
        return e[...] * (jnp.exp(st[q, slot, 0:1, :] - top) / total)

    def consume(q):
        top, total = gather_stats(q)
        post = weigh(q, me_t, e_ref.at[q], top, total)
        occ[...] += jnp.sum(post, axis=1, keepdims=True)
        post_ref[q] = post.astype(jnp.bfloat16)
        return top, total

    bits = [1 << k for k in range(n_img.bit_length() - 1)]
    groups = len(bits) if bits and tpl_rows % (16 * len(bits)) == 0 else 1
    depth = tpl_rows // groups
    orders = [bits[g:] + bits[:g] for g in range(groups)]
    masks = sorted(range(1, n_img), key=lambda mask: -mask.bit_count())

    def flip(mask):
        return me_i + sum(b - 2 * b * lax.rem(lax.div(me_i, b), 2) for b in bits if b & mask)

    def turn(g, mask):
        return next(r for r, b in enumerate(orders[g]) if b & mask)

    def band(g):
        return slice(g * depth, (g + 1) * depth)

    def part_of(mask):
        return pl.ds(pl.multiple_of(flip(mask) * cols, cols), cols)

    class Reduction:
        def __init__(self, src, dst, sent, got, share):
            self.src, self.dst, self.sent, self.got, self.share = src, dst, sent, got, share

        def copy(self, g, mask):
            return pltpu.make_async_remote_copy(
                src_ref=self.src.at[mask, band(g)], dst_ref=self.dst.at[mask, band(g)],
                send_sem=self.sent.at[g, mask], recv_sem=self.got.at[g, mask],
                device_id={"img": flip(orders[g][turn(g, mask)])}, device_id_type=MESH)

        def received(self, g, mask, rounds):
            value = 0.0
            for b in orders[g][:rounds]:
                self.copy(g, b + mask).wait_recv()
                value += self.dst[b + mask, band(g)].astype(jnp.float32)
            return value

        def round(self, r):
            for mask in masks:
                for g in range(groups):
                    if turn(g, mask) == r:
                        value = self.share(g, mask)
                        self.src[mask, band(g)] = (value + self.received(g, mask, r)).astype(jnp.bfloat16)
                        self.copy(g, mask).start()

        def drain(self):
            for mask in masks:
                for g in range(groups):
                    self.copy(g, mask).wait_send()

    def share_end(g, mask):
        block = imgs[pl.ds(2 * chip, 2), :, part_of(mask)].reshape(2 * rows, cols)
        return jnp.dot(post_end[band(g)], block, preferred_element_type=jnp.float32)

    reduce_end = Reduction(sbuf_end, rbuf_end, ers_send, ers_recv, share_end)

    def row_of(column):
        return jnp.transpose(jnp.broadcast_to(column, (tpl_rows, 128)))[0:8]

    def hand_occ():
        return pltpu.make_async_remote_copy(
            src_ref=obuf_end, dst_ref=orecv_end, send_sem=hand_send.at[0],
            recv_sem=hand_recv.at[0], device_id={"tpl": outer}, device_id_type=MESH)

    def hand_evidence(q):
        return pltpu.make_async_remote_copy(
            src_ref=le_row.at[q], dst_ref=le_row.at[q], send_sem=hand_send.at[1],
            recv_sem=hand_recv.at[1], device_id={"tpl": outer}, device_id_type=MESH)

    def hand_sum(g):
        return pltpu.make_async_remote_copy(
            src_ref=zsend.at[band(g)], dst_ref=zrecv.at[band(g)], send_sem=z_send.at[g],
            recv_sem=z_recv.at[g], device_id={"tpl": outer}, device_id_type=MESH)

    def hub_spread(k):
        end_arrival(me_i, k).wait_recv()
        for off in range(1, n_img):
            spread_copy(off, k).start()

    def hub_score():
        for off in range(1, n_img):
            for k in range(t_parts):
                end_arrival(img_peer(off), k).wait_recv()
        sqn_end[...] = half_norm(et_ref)
        score(chip, end_slot, et_ref, sqn_end, e_end)
        tell(chip, end_slot, est_send)

    def hub_consume():
        top, total = consume(chip)
        post = weigh(chip, end_slot, e_end, top, total)
        obuf_end[...] = row_of(jnp.sum(post, axis=1, keepdims=True))
        post_end[...] = post.astype(jnp.bfloat16)
        reduce_end.round(0)
        hand_occ().start()
        hand_evidence(chip).start()

    def middle(q, carry):
        @pl.when(jnp.logical_not(jnp.logical_or(absent(q, chip), is_hub & (q == chip))))
        def _():
            consume(q)

        @pl.when(jnp.logical_not(absent(q, chip)))
        def _():
            for j in range(n_img):
                part = slice(j * cols, (j + 1) * cols)
                block = imgs[pl.ds(2 * q, 2), :, part].reshape(2 * rows, cols)
                acc[:, part] += jnp.dot(post_ref[q], block, preferred_element_type=jnp.float32)

        return carry

    def middles():
        lax.fori_loop(1, chips - 1, middle, 0)

    finish(chip)
    n_far = last - rank - skip
    late = parts // 2 if hubs else 0

    def arrive(b, carry):
        q_far = chip + inward * (b + 1 + skip)

        def near_event(block, k):
            q_near = chip - inward * (block + 1)
            there = jnp.logical_and(block >= 0, block < rank)

            @pl.when(there)
            def _():
                relay(q_near, k, last > 0, 0, inner)

            if k == parts - 1:
                @pl.when(there)
                def _():
                    finish(q_near)

        for k in range(parts):
            @pl.when(b < n_far)
            def _():
                relay(q_far, k, rank > 0, 1, outer)

            if k >= late:
                near_event(b, k - late)
            else:
                near_event(b - 1, k - late + parts)
            if hubs:
                spreads = [j for j in range(t_parts) if k == min(j + 1, parts - 1)]
                if spreads:
                    @pl.when(jnp.logical_and(is_hub, b == 0))
                    def _():
                        for j in spreads:
                            hub_spread(j)

                if k == parts // 2:
                    @pl.when(jnp.logical_and(is_end, b == n_far - 1))
                    def _():
                        middles()

                steps = ((parts // 3 - 1, hub_score), (parts // 2, hub_consume))
                due = [step for at, step in steps if k == max(0, min(at, parts - 1))]
                if due:
                    @pl.when(jnp.logical_and(is_hub, b == 1))
                    def _():
                        for step in due:
                            step()

        final = q_far == opposite

        @pl.when(jnp.logical_and(b < n_far, jnp.logical_not(is_end & final)))
        def _():
            finish(q_far)

        if hubs:
            @pl.when((b < n_far) & is_hub & final)
            def _():
                score(q_far, end_slot, et_ref, sqn_end, None)
                tell(q_far, end_slot, est_send)

            @pl.when((b < n_far) & is_end & final)
            def _():
                finish_given(q_far)

        return carry

    lax.fori_loop(0, last - 1 if hubs else last, arrive, 0)

    if hubs:
        @pl.when(is_hub)
        def _():
            for r in range(1, len(bits)):
                reduce_end.round(r)
            for g in range(groups):
                own_end[band(g)] = share_end(g, 0)

    @pl.when(jnp.logical_not(is_end))
    def _():
        middles()

    ends = (0, chips - 1) if chips > 1 else (0,)
    for q in ends:
        consume(q)

    def occ_copy(off):
        return pltpu.make_async_remote_copy(
            src_ref=obuf, dst_ref=orecv.at[off], send_sem=oc_send.at[off],
            recv_sem=oc_recv.at[off], device_id={"img": img_peer(off)}, device_id_type=MESH)

    def share(g, mask):
        part = part_of(mask)
        value = acc[band(g), part]
        for q in ends:
            block = imgs[2 * q:2 * q + 2, :, part].reshape(2 * rows, cols)
            value += jnp.dot(post_ref[q, band(g)], block, preferred_element_type=jnp.float32)
        return value

    reduce_own = Reduction(sbuf, rbuf, rs_send, rs_recv, share)
    obuf[...] = row_of(occ[...])
    if hubs:
        @pl.when(is_end)
        def _():
            hand_occ().wait_recv()
            hand_evidence(chip + inward).wait_recv()
            obuf[...] += orecv_end[...]

    for off in range(1, n_img):
        occ_copy(off).start()
    for q in range(chips):
        le_ref[:, q * pair:(q + 1) * pair] = le_row[q]
    mine = part_of(0)
    for r in range(len(bits)):
        reduce_own.round(r)
        if r == 0:
            if hubs:
                @pl.when(is_hub)
                def _():
                    for g in range(groups):
                        zsend[band(g)] = (own_end[band(g)] + reduce_end.received(g, 0, len(bits))).astype(jnp.bfloat16)
                        hand_sum(g).start()

            for g in range(groups):
                own[band(g)] = share(g, 0) + t_ref[band(g), mine].astype(jnp.float32)
            occ_row = obuf[...]
            for off in range(1, n_img):
                occ_copy(off).wait_recv()
                occ_row += orecv[off]
            occ_col = jnp.transpose(jnp.broadcast_to(occ_row[0:1], (128, tpl_rows)))[:, 0:1]
            occ[...] = occ_col + 1.0
    if hubs:
        @pl.when(is_end)
        def _():
            for g in range(groups):
                hand_sum(g).wait_recv()
                own[band(g)] += zrecv[band(g)].astype(jnp.float32)

    for g in range(groups):
        out_ref[band(g)] = (own[band(g)] + reduce_own.received(g, 0, len(bits))) / occ[band(g)]

    for off in range(1, n_img):
        occ_copy(off).wait_send()
    reduce_own.drain()
    if hubs:
        @pl.when(is_end)
        def _():
            for k in range(t_parts):
                end_copy(k).wait_send()

        @pl.when(is_hub)
        def _():
            for off in range(1, n_img):
                for k in range(t_parts):
                    spread_copy(off, k).wait_send()
            told(chip, end_slot, est_send)
            told(opposite, end_slot, est_send)
            hand_occ().wait_send()
            hand_evidence(chip).wait_send()
            reduce_end.drain()
            for g in range(groups):
                hand_sum(g).wait_send()

    def drain(q, carry):
        block = 2 * q + core
        away = (q - chip) * inward
        goes_out = (rank > 0) & (away >= 0) & jnp.logical_not(is_hub & (away == 0))
        for k in range(parts):
            @pl.when((away <= 0) & (last > 0))
            def _():
                image_copy(imgs.at[block], block, k, 0, inner).wait_send()

            @pl.when(goes_out)
            def _():
                image_copy(imgs.at[block], block, k, 1, outer).wait_send()

            @pl.when(jnp.logical_not(absent(q, chip)))
            def _():
                image_copy(imgs.at[block], block, k, 2, sibling).wait_send()

        @pl.when(jnp.logical_not(jnp.logical_or(absent(q, chip), is_end & (q == opposite))))
        def _():
            told(q, me_t, st_send)

        return carry

    lax.fori_loop(0, chips, drain, 0)


def emit(new_ref, evidence_ref, new_out, evidence_out, sem):
    move = pltpu.make_async_copy(new_ref, new_out, sem)
    move.start()
    evidence_out[...] = evidence_ref[...].reshape(evidence_out.shape)
    move.wait()


def solution(mesh):
    n_img, n_tpl = mesh.shape["img"], mesh.shape["tpl"]
    chips = n_tpl // 2

    def per_device(images, templates, class_exponent, class_mask):
        rows, feats = images.shape
        tpl_rows = templates.shape[0]
        cols = feats // n_img
        class_count = class_exponent.shape[0]
        parts = max(c for c in (6, 3, 2, 1) if rows % (16 * c) == 0 or c == 1)
        dma = pltpu.SemaphoreType.DMA
        vmem = pl.BlockSpec(memory_space=pltpu.VMEM)
        far = pl.BlockSpec(memory_space=pl.ANY)
        new, evidence = pl.pallas_call(
            functools.partial(kernel, n_img, n_tpl, parts),
            out_shape=(
                pltpu.VMEM((tpl_rows, cols), jnp.float32),
                pltpu.VMEM((1, n_tpl * rows), jnp.float32),
            ),
            in_specs=[far, far, pl.BlockSpec(memory_space=pltpu.SMEM), far],
            out_specs=(vmem, vmem),
            scratch_shapes=[
                pltpu.VMEM((tpl_rows, feats), jnp.bfloat16),
                pltpu.VMEM((class_count, n_tpl * rows), jnp.int32),
                dma((3,)),
                pltpu.VMEM((n_tpl, rows, feats), jnp.bfloat16),
                pltpu.VMEM((chips, class_count, 2 * rows), jnp.int32),
                pltpu.VMEM((chips, 1, 2 * rows), jnp.float32),
                pltpu.VMEM((chips, tpl_rows, 2 * rows), jnp.float32),
                pltpu.VMEM((chips, tpl_rows, 2 * rows), jnp.bfloat16),
                pltpu.VMEM((chips, n_tpl, 2, 2 * rows), jnp.float32),
                pltpu.VMEM((tpl_rows, feats), jnp.float32),
                pltpu.VMEM((tpl_rows, cols), jnp.float32),
                pltpu.VMEM((n_img, tpl_rows, cols), jnp.bfloat16),
                pltpu.VMEM((n_img, tpl_rows, cols), jnp.bfloat16),
                pltpu.VMEM((tpl_rows, 1), jnp.float32),
                pltpu.VMEM((tpl_rows, 1), jnp.float32),
                pltpu.VMEM((8, tpl_rows), jnp.float32),
                pltpu.VMEM((n_img, 8, tpl_rows), jnp.float32),
                dma((3, chips, parts)),
                dma((n_tpl, parts)),
                dma((chips, n_tpl)),
                dma((chips, n_tpl)),
                dma((n_img, n_img)),
                dma((n_img, n_img)),
                dma((n_img,)),
                dma((n_img,)),
                pltpu.VMEM((tpl_rows, feats), jnp.bfloat16),
                pltpu.VMEM((tpl_rows, 2 * rows), jnp.float32),
                pltpu.VMEM((tpl_rows, 2 * rows), jnp.bfloat16),
                pltpu.VMEM((tpl_rows, 1), jnp.float32),
                pltpu.VMEM((tpl_rows, 1), jnp.float32),
                pltpu.VMEM((tpl_rows, cols), jnp.float32),
                pltpu.VMEM((n_img, tpl_rows, cols), jnp.bfloat16),
                pltpu.VMEM((n_img, tpl_rows, cols), jnp.bfloat16),
                pltpu.VMEM((tpl_rows, cols), jnp.bfloat16),
                pltpu.VMEM((tpl_rows, cols), jnp.bfloat16),
                pltpu.VMEM((8, tpl_rows), jnp.float32),
                pltpu.VMEM((8, tpl_rows), jnp.float32),
                dma((n_img, 2)),
                dma((n_img, 2)),
                dma((chips, n_tpl)),
                dma((n_img, n_img)),
                dma((n_img, n_img)),
                dma((n_img,)),
                dma((n_img,)),
                dma((2,)),
                dma((2,)),
            ],
            compiler_params=pltpu.CompilerParams(
                collective_id=0, has_side_effects=True, vmem_limit_bytes=60 * 1024 * 1024),
        )(images, templates, class_exponent, class_mask.T)
        return pl.pallas_call(
            emit,
            out_shape=(
                jax.ShapeDtypeStruct(new.shape, jnp.float32),
                jax.ShapeDtypeStruct((n_tpl * rows,), jnp.float32),
            ),
            in_specs=[vmem] * 2,
            out_specs=(far, vmem),
            scratch_shapes=[dma],
        )(*[pltpu.with_memory_space_constraint(x, pltpu.VMEM) for x in (new, evidence)])

    in_specs = (P(("img", "tpl"), None), P("tpl", None), P(), P("img", None))
    out_specs = (P("tpl", "img"), P("img"))
    return jax.shard_map(
        per_device, mesh=mesh, in_specs=in_specs, out_specs=out_specs, check_vma=False
    )
```

```python
import functools

import jax
import jax.numpy as jnp
from jax import lax
from jax.experimental import pallas as pl
from jax.experimental.pallas import tpu as pltpu
from jax.sharding import PartitionSpec as P

MESH = pl.DeviceIdType.MESH
floor_score = -1e30


def kernel(
    n_img, n_tpl, parts, x_ref, t_hbm, power_ref, mask_hbm, out_ref, le_ref,
    t_ref, mask_ref, loads, imgs, allow, le_row, e_ref, post_ref, st, acc, own, sbuf, rbuf, sqn, occ, obuf, orecv,
    img_send, img_recv, st_send, st_recv, rs_send, rs_recv, oc_send, oc_recv,
    here, there, et_ref, e_end, post_end, sqn_end, occ_end, own_end, sbuf_end, rbuf_end, zsend, zrecv, obuf_end, orecv_end,
    et_send, et_recv, est_send, ers_send, ers_recv, z_send, z_recv, hand_send, hand_recv,
):
    chips = n_tpl // 2
    last = chips - 1
    hubs = chips >= 4
    rows, feats = x_ref.shape
    cols = feats // n_img
    me_i, me_t = lax.axis_index("img"), lax.axis_index("tpl")
    chip, core = lax.div(me_t, 2), lax.rem(me_t, 2)
    sibling = 2 * chip + 1 - core
    side = lax.div(2 * chip, chips)
    inward = 1 - 2 * side
    rank = chip + side * (last - 2 * chip)
    inner, outer = me_t + 2 * inward, me_t - 2 * inward
    is_end = jnp.logical_and(rank == 0, hubs)
    is_hub = jnp.logical_and(rank == 1, hubs)
    skip = jnp.where(is_end, 1, 0)
    end_slot = outer
    opposite = last * (1 - side)

    def absent(q, who):
        if not hubs:
            return False
        low = jnp.logical_and(q == 1, who == 0)
        return jnp.logical_or(low, jnp.logical_and(q == last - 1, who == last))

    def tpl_peer(off):
        return lax.rem(me_t + off, n_tpl)

    def img_peer(off):
        return lax.rem(me_i + off, n_img)

    barrier = pltpu.get_barrier_semaphore()
    for off in range(1, n_tpl):
        pl.semaphore_signal(barrier, inc=1, device_id={"tpl": tpl_peer(off)}, device_id_type=MESH)
    for off in range(1, n_img):
        pl.semaphore_signal(barrier, inc=1, device_id={"img": img_peer(off)}, device_id_type=MESH)
    load_t = pltpu.make_async_copy(t_hbm, t_ref, loads.at[0])
    load_x = pltpu.make_async_copy(x_ref, imgs.at[me_t], loads.at[1])
    load_mask = pltpu.make_async_copy(mask_hbm, mask_ref, loads.at[2])
    for load in (load_t, load_x, load_mask):
        load.start()
    pl.semaphore_wait(barrier, n_tpl - 1 + n_img - 1)

    size = rows // parts
    tpl_rows = t_ref.shape[0]
    quarter = tpl_rows // n_img
    t_parts = 2 if quarter % 32 == 0 else 1
    t_size = quarter // t_parts

    pair = 2 * rows
    ahead = 2 * rows // 3
    split = hubs and parts % 3 == 0 and ahead % 128 == 0 and pair == 3 * ahead
    early = ((0, ahead), (pair - ahead, pair)) if split else ()
    late_lanes = ((ahead, pair - ahead),) if split else ((0, pair),)

    def image_copy(src, block, k, way, to):
        place = k + lax.rem(block, 2) * (parts - 1 - 2 * k) if split else k
        piece = pl.ds(pl.multiple_of(place * size, size), size)
        return pltpu.make_async_remote_copy(
            src_ref=src.at[piece], dst_ref=imgs.at[block, piece],
            send_sem=img_send.at[way, lax.div(block, 2), k],
            recv_sem=img_recv.at[block, k], device_id={"tpl": to}, device_id_type=MESH)

    def share_rows(owner, k):
        return pl.ds(owner * quarter + k * t_size, t_size)

    def end_copy(k):
        piece = share_rows(me_i, k)
        return pltpu.make_async_remote_copy(
            src_ref=t_hbm.at[piece], dst_ref=et_ref.at[piece], send_sem=et_send.at[0, k],
            recv_sem=et_recv.at[me_i, k], device_id={"tpl": inner}, device_id_type=MESH)

    def spread_copy(off, k):
        piece = share_rows(me_i, k)
        return pltpu.make_async_remote_copy(
            src_ref=et_ref.at[piece], dst_ref=et_ref.at[piece], send_sem=et_send.at[off, k],
            recv_sem=et_recv.at[me_i, k], device_id={"img": img_peer(off)}, device_id_type=MESH)

    def end_arrival(owner, k):
        piece = share_rows(owner, k)
        return pltpu.make_async_remote_copy(
            src_ref=et_ref.at[piece], dst_ref=et_ref.at[piece], send_sem=et_send.at[0, k],
            recv_sem=et_recv.at[owner, k], device_id={"img": img_peer(1)}, device_id_type=MESH)

    own_block = 2 * chip + core
    sends_out = jnp.logical_and(rank > 0, jnp.logical_not(is_hub))
    if hubs:
        @pl.when(is_end)
        def _():
            for k in range(t_parts):
                end_copy(k).start()

    for k in range(parts):
        if chips > 1:
            image_copy(x_ref, own_block, k, 0, inner).start()

        @pl.when(sends_out)
        def _():
            image_copy(x_ref, own_block, k, 1, outer).start()

        image_copy(x_ref, own_block, k, 2, sibling).start()

    for load in (load_t, load_x, load_mask):
        load.wait()

    def half_norm(ref):
        tf = ref[...].astype(jnp.float32)
        return 0.5 * jnp.sum(tf * tf, axis=1, keepdims=True)

    sqn[...] = half_norm(t_ref)
    acc[...] = jnp.zeros_like(acc)
    occ[...] = jnp.zeros_like(occ)

    def stat_copy(q, slot, off, sems):
        return pltpu.make_async_remote_copy(
            src_ref=st.at[q, slot], dst_ref=st.at[q, slot], send_sem=sems.at[q, off],
            recv_sem=st_recv.at[q, slot], device_id={"tpl": tpl_peer(off)}, device_id_type=MESH)

    def stat_arrival(q, slot):
        return pltpu.make_async_remote_copy(
            src_ref=st.at[q, slot], dst_ref=st.at[q, slot], send_sem=st_send.at[q, 0],
            recv_sem=st_recv.at[q, slot], device_id={"tpl": tpl_peer(1)}, device_id_type=MESH)

    def tell(q, slot, sems):
        for off in range(1, n_tpl):
            @pl.when(jnp.logical_not(absent(q, lax.div(tpl_peer(off), 2))))
            def _():
                stat_copy(q, slot, off, sems).start()

    def told(q, slot, sems):
        for off in range(1, n_tpl):
            @pl.when(jnp.logical_not(absent(q, lax.div(tpl_peer(off), 2))))
            def _():
                stat_copy(q, slot, off, sems).wait_send()

    def pair_of(q):
        return imgs[pl.ds(2 * q, 2)].reshape(2 * rows, feats)

    def images_of(q, lanes):
        cuts = [(c, max(lo - c * rows, 0), min(hi - c * rows, rows)) for lo, hi in lanes for c in range(2)]
        return jnp.concatenate([imgs[2 * q + c, lo:hi] for c, lo, hi in cuts if lo < hi])

    class_count = power_ref.shape[0]
    per_class = tpl_rows * n_tpl // class_count
    for q in range(chips):
        allow[q] = mask_ref[:, q * pair:(q + 1) * pair]

    def inverse_temp(c):
        power = jnp.full((1, pair), power_ref[c], jnp.int32)
        return 0.5 * jnp.exp2(0.5 * power.astype(jnp.float32))

    def class_terms(slot, q, lanes):
        first = slot * tpl_rows
        width = sum(hi - lo for lo, hi in lanes)

        def mask_of(c):
            row = allow[q, pl.ds(c, 1), :]
            return jnp.concatenate([row[:, lo:hi] for lo, hi in lanes], axis=1)

        if per_class % tpl_rows == 0:
            only = lax.div(first, per_class)
            return inverse_temp(only)[:, :width], mask_of(only) > 0
        owner = lax.div(first + lax.broadcasted_iota(jnp.int32, (tpl_rows, width), 0), per_class)
        beta = sum(jnp.where(owner == c, inverse_temp(c)[:, :width], 0.0) for c in range(class_count))
        return beta, sum(jnp.where(owner == c, mask_of(c), 0) for c in range(class_count)) > 0

    def score(q, slot, tpl, norm, e_out, tops, totals, lanes=None):
        images = pair_of(q) if lanes is None else images_of(q, lanes)
        lanes = lanes or ((0, pair),)
        raw = lax.dot_general(
            tpl[...], images, (((1,), (1,)), ((), ())), preferred_element_type=jnp.float32)
        beta, allowed = class_terms(slot, q, lanes)
        s = beta * (raw - norm[...])
        top = jnp.max(jnp.where(allowed, s, floor_score), axis=0, keepdims=True)
        e = jnp.where(allowed, jnp.exp(s - top), 0.0)
        total = jnp.sum(e, axis=0, keepdims=True)
        at = 0
        for lo, hi in lanes:
            tops[:, lo:hi] = top[:, at:at + hi - lo]
            totals[:, lo:hi] = total[:, at:at + hi - lo]
            if e_out is not None:
                e_out[:, lo:hi] = e[:, at:at + hi - lo]
            at += hi - lo

    def own_score(q, lanes=None):
        score(q, me_t, t_ref, sqn, e_ref.at[q], here.at[q, 0], here.at[q, 1], lanes)

    def end_score(q, lanes=None):
        score(q, end_slot, et_ref, sqn_end, e_end if q is chip else None, there.at[0], there.at[1], lanes)

    def put_stats(q):
        st[q, me_t, 0:1, :] = here[q, 0]
        st[q, me_t, 1:2, :] = here[q, 1]

    def put_joint_stats(q):
        top = jnp.maximum(here[q, 0], there[0])
        st[q, me_t, 0:1, :] = top
        st[q, me_t, 1:2, :] = here[q, 1] * jnp.exp(here[q, 0] - top) + there[1] * jnp.exp(there[0] - top)

    def wait_image(block, k):
        image_copy(imgs.at[block], block, k, 2, sibling).wait_recv()

    def relay(q, k, more, way, to):
        block = 2 * q + core
        wait_image(block, k)

        @pl.when(more)
        def _():
            image_copy(imgs.at[block], block, k, way, to).start()

        image_copy(imgs.at[block], block, k, 2, sibling).start()

    def wait_sibling(q):
        for k in range(parts):
            wait_image(2 * q + 1 - core, k)

    def finish(q):
        wait_sibling(q)
        own_score(q)
        put_stats(q)
        tell(q, me_t, st_send)

    def ready(k):
        return k == 2 * parts // 3

    def finish_ahead(q):
        for k in range(2 * parts // 3):
            wait_image(2 * q + 1 - core, k)
        own_score(q, early)

        @pl.when(is_hub)
        def _():
            end_score(q, early)

    def finish_last(q):
        for k in range(2 * parts // 3 if split else 0, parts):
            wait_image(2 * q + 1 - core, k)
        own_score(q, late_lanes)

        @pl.when(is_hub)
        def _():
            end_score(q, late_lanes)
            put_joint_stats(q)
            tell(q, me_t, st_send)

    def mute(q, who):
        if not hubs:
            return False
        low = jnp.logical_and(q == last, who == 0)
        return jnp.logical_or(low, jnp.logical_and(q == 0, who == last))

    def gather_stats(q):
        for off in range(1, n_tpl):
            slot = tpl_peer(off)
            silent = jnp.logical_or(is_hub & (q == chip) & (slot == end_slot), mute(q, lax.div(slot, 2)))

            @pl.when(jnp.logical_not(silent))
            def _():
                stat_arrival(q, slot).wait_recv()

        heard = range(n_tpl)
        if hubs and isinstance(q, int):
            heard = [j for j in heard if not (q == last and j < 2) and not (q == 0 and j >= 2 * last)]
        tops = {j: st[q, j, 0:1, :] for j in heard}
        top = functools.reduce(jnp.maximum, tops.values())
        total = sum(st[q, j, 1:2, :] * jnp.exp(tops[j] - top) for j in heard)
        le_row[q] = top + jnp.log(total)
        return top, total

    def weigh(e, local, top, total):
        return e[...] * (jnp.exp(local - top) / total)

    def consume(q, count=True):
        top, total = gather_stats(q)
        post = weigh(e_ref.at[q], here[q, 0], top, total)
        post_ref[q] = post.astype(jnp.bfloat16)
        if count:
            occ[...] += jnp.sum(post, axis=1, keepdims=True)
        else:
            e_ref[q] = post
        return top, total

    bits = [1 << k for k in range(n_img.bit_length() - 1)]
    groups = len(bits) if bits and tpl_rows % (16 * len(bits)) == 0 else 1
    depth = tpl_rows // groups
    orders = [bits[g:] + bits[:g] for g in range(groups)]
    masks = sorted(range(1, n_img), key=lambda mask: -mask.bit_count())

    def flip(mask):
        return me_i + sum(b - 2 * b * lax.rem(lax.div(me_i, b), 2) for b in bits if b & mask)

    def turn(g, mask):
        return next(r for r, b in enumerate(orders[g]) if b & mask)

    def band(g):
        return slice(g * depth, (g + 1) * depth)

    def part_of(mask):
        return pl.ds(pl.multiple_of(flip(mask) * cols, cols), cols)

    class Reduction:
        def __init__(self, src, dst, sent, got, share):
            self.src, self.dst, self.sent, self.got, self.share = src, dst, sent, got, share

        def copy(self, g, mask):
            return pltpu.make_async_remote_copy(
                src_ref=self.src.at[mask, band(g)], dst_ref=self.dst.at[mask, band(g)],
                send_sem=self.sent.at[g, mask], recv_sem=self.got.at[g, mask],
                device_id={"img": flip(orders[g][turn(g, mask)])}, device_id_type=MESH)

        def received(self, g, mask, rounds):
            value = 0.0
            for b in orders[g][:rounds]:
                self.copy(g, b + mask).wait_recv()
                value += self.dst[b + mask, band(g)].astype(jnp.float32)
            return value

        def round(self, r):
            for mask in masks:
                for g in range(groups):
                    if turn(g, mask) == r:
                        value = self.share(g, mask)
                        self.src[mask, band(g)] = (value + self.received(g, mask, r)).astype(jnp.bfloat16)
                        self.copy(g, mask).start()

        def drain(self):
            for mask in masks:
                for g in range(groups):
                    self.copy(g, mask).wait_send()

    def share_end(g, mask):
        block = imgs[pl.ds(2 * chip, 2), :, part_of(mask)].reshape(2 * rows, cols)
        return jnp.dot(post_end[band(g)], block, preferred_element_type=jnp.float32)

    reduce_end = Reduction(sbuf_end, rbuf_end, ers_send, ers_recv, share_end)

    def row_of(column):
        return jnp.transpose(jnp.broadcast_to(column, (tpl_rows, 128)))[0:8]

    def hand_occ():
        return pltpu.make_async_remote_copy(
            src_ref=obuf_end, dst_ref=orecv_end, send_sem=hand_send.at[0],
            recv_sem=hand_recv.at[0], device_id={"tpl": outer}, device_id_type=MESH)

    def hand_evidence(q):
        return pltpu.make_async_remote_copy(
            src_ref=le_row.at[q], dst_ref=le_row.at[q], send_sem=hand_send.at[1],
            recv_sem=hand_recv.at[1], device_id={"tpl": outer}, device_id_type=MESH)

    def hand_sum(g):
        return pltpu.make_async_remote_copy(
            src_ref=zsend.at[band(g)], dst_ref=zrecv.at[band(g)], send_sem=z_send.at[g],
            recv_sem=z_recv.at[g], device_id={"tpl": outer}, device_id_type=MESH)

    def hub_spread(k):
        end_arrival(me_i, k).wait_recv()
        for off in range(1, n_img):
            spread_copy(off, k).start()

    def hub_score():
        for off in range(1, n_img):
            for k in range(t_parts):
                end_arrival(img_peer(off), k).wait_recv()
        sqn_end[...] = half_norm(et_ref)
        end_score(chip)
        st[chip, end_slot, 0:1, :] = there[0]
        st[chip, end_slot, 1:2, :] = there[1]
        tell(chip, end_slot, est_send)

    def hub_consume():
        top, total = consume(chip)
        post = weigh(e_end, there[0], top, total)
        obuf_end[...] = row_of(jnp.sum(post, axis=1, keepdims=True))
        post_end[...] = post.astype(jnp.bfloat16)
        reduce_end.round(0)
        hand_occ().start()
        hand_evidence(chip).start()

    def middle(q, carry):
        @pl.when(jnp.logical_not(jnp.logical_or(absent(q, chip), is_hub & (q == chip))))
        def _():
            consume(q)

        @pl.when(jnp.logical_not(absent(q, chip)))
        def _():
            for j in range(n_img):
                part = slice(j * cols, (j + 1) * cols)
                block = imgs[pl.ds(2 * q, 2), :, part].reshape(2 * rows, cols)
                acc[:, part] += jnp.dot(post_ref[q], block, preferred_element_type=jnp.float32)

        return carry

    def middles():
        lax.fori_loop(1, chips - 1, middle, 0)

    finish(chip)
    n_far = last - rank - skip
    late = parts // 2 if hubs else 0

    def arrive(b, carry):
        q_far = chip + inward * (b + 1 + skip)

        def near_event(block, k):
            q_near = chip - inward * (block + 1)
            there = jnp.logical_and(block >= 0, block < rank)

            @pl.when(there)
            def _():
                relay(q_near, k, last > 0, 0, inner)

            if k == parts - 1:
                @pl.when(there)
                def _():
                    finish(q_near)

        for k in range(parts):
            @pl.when(b < n_far)
            def _():
                relay(q_far, k, rank > 0, 1, outer)

            if split and ready(k):
                @pl.when(jnp.logical_or(is_end, is_hub) & (b < n_far) & (q_far == opposite))
                def _():
                    finish_ahead(q_far)

            if k >= late:
                near_event(b, k - late)
            else:
                near_event(b - 1, k - late + parts)
            if hubs:
                spreads = [j for j in range(t_parts) if k == min(j + 1, parts - 1)]
                if spreads:
                    @pl.when(jnp.logical_and(is_hub, b == 0))
                    def _():
                        for j in spreads:
                            hub_spread(j)

                if k == parts // 2:
                    @pl.when(jnp.logical_and(is_end, b == n_far - 1))
                    def _():
                        middles()

                steps = ((parts // 3 - 1, hub_score), (parts // 2, hub_consume))
                due = [step for at, step in steps if k == max(0, min(at, parts - 1))]
                if due:
                    @pl.when(jnp.logical_and(is_hub, b == 1))
                    def _():
                        for step in due:
                            step()

        speaks = jnp.logical_or(is_end, is_hub) & (q_far == opposite)

        @pl.when(jnp.logical_and(b < n_far, jnp.logical_not(speaks)))
        def _():
            finish(q_far)

        if hubs:
            @pl.when(jnp.logical_and(b < n_far, speaks))
            def _():
                finish_last(q_far)

        return carry

    lax.fori_loop(0, last - 1 if hubs else last, arrive, 0)

    if hubs:
        @pl.when(is_hub)
        def _():
            for r in range(1, len(bits)):
                reduce_end.round(r)
            for g in range(groups):
                own_end[band(g)] = share_end(g, 0)

    @pl.when(jnp.logical_not(is_end))
    def _():
        middles()

    ends = (0, chips - 1) if chips > 1 else (0,)
    for q in ends:
        consume(q, count=False)

    def occ_copy(off):
        return pltpu.make_async_remote_copy(
            src_ref=obuf, dst_ref=orecv.at[off], send_sem=oc_send.at[off],
            recv_sem=oc_recv.at[off], device_id={"img": img_peer(off)}, device_id_type=MESH)

    def share(g, mask):
        part = part_of(mask)
        value = acc[band(g), part]
        for q in ends:
            block = imgs[2 * q:2 * q + 2, :, part].reshape(2 * rows, cols)
            value += jnp.dot(post_ref[q, band(g)], block, preferred_element_type=jnp.float32)
        return value

    reduce_own = Reduction(sbuf, rbuf, rs_send, rs_recv, share)
    mine = part_of(0)
    for r in range(len(bits)):
        reduce_own.round(r)
        if r == 0:
            for q in ends:
                occ[...] += jnp.sum(e_ref[q], axis=1, keepdims=True)
            obuf[...] = row_of(occ[...])
            if hubs:
                @pl.when(is_end)
                def _():
                    hand_occ().wait_recv()
                    hand_evidence(chip + inward).wait_recv()
                    obuf[...] += orecv_end[...]

            for off in range(1, n_img):
                occ_copy(off).start()
            for q in range(chips):
                le_ref[:, q * pair:(q + 1) * pair] = le_row[q]
            if hubs:
                @pl.when(is_hub)
                def _():
                    for g in range(groups):
                        zsend[band(g)] = (own_end[band(g)] + reduce_end.received(g, 0, len(bits))).astype(jnp.bfloat16)
                        hand_sum(g).start()

            for g in range(groups):
                own[band(g)] = share(g, 0) + t_ref[band(g), mine].astype(jnp.float32)
    if hubs:
        @pl.when(is_end)
        def _():
            for k in range(t_parts):
                end_copy(k).wait_send()

        @pl.when(is_hub)
        def _():
            for off in range(1, n_img):
                for k in range(t_parts):
                    spread_copy(off, k).wait_send()
            told(chip, end_slot, est_send)
            hand_occ().wait_send()
            hand_evidence(chip).wait_send()
            reduce_end.drain()

    def drain(q, carry):
        block = 2 * q + core
        away = (q - chip) * inward
        goes_out = (rank > 0) & (away >= 0) & jnp.logical_not(is_hub & (away == 0))
        for k in range(parts):
            @pl.when((away <= 0) & (last > 0))
            def _():
                image_copy(imgs.at[block], block, k, 0, inner).wait_send()

            @pl.when(goes_out)
            def _():
                image_copy(imgs.at[block], block, k, 1, outer).wait_send()

            @pl.when(jnp.logical_not(absent(q, chip)))
            def _():
                image_copy(imgs.at[block], block, k, 2, sibling).wait_send()

        @pl.when(jnp.logical_not(jnp.logical_or(absent(q, chip), is_end & (q == opposite))))
        def _():
            told(q, me_t, st_send)

        return carry

    lax.fori_loop(0, chips, drain, 0)

    occ_row = obuf[...]
    for off in range(1, n_img):
        occ_copy(off).wait_recv()
        occ_row += orecv[off]
    occ_col = jnp.transpose(jnp.broadcast_to(occ_row[0:1], (128, tpl_rows)))[:, 0:1]
    occ[...] = occ_col + 1.0

    if hubs:
        @pl.when(is_end)
        def _():
            for g in range(groups):
                hand_sum(g).wait_recv()
                own[band(g)] += zrecv[band(g)].astype(jnp.float32)

    for g in range(groups):
        out_ref[band(g)] = (own[band(g)] + reduce_own.received(g, 0, len(bits))) / occ[band(g)]

    for off in range(1, n_img):
        occ_copy(off).wait_send()
    reduce_own.drain()
    if hubs:
        @pl.when(is_hub)
        def _():
            for g in range(groups):
                hand_sum(g).wait_send()


def emit(new_ref, evidence_ref, new_out, evidence_out, sem):
    move = pltpu.make_async_copy(new_ref, new_out, sem)
    move.start()
    evidence_out[...] = evidence_ref[...].reshape(evidence_out.shape)
    move.wait()


def solution(mesh):
    n_img, n_tpl = mesh.shape["img"], mesh.shape["tpl"]
    chips = n_tpl // 2

    def per_device(images, templates, class_exponent, class_mask):
        rows, feats = images.shape
        tpl_rows = templates.shape[0]
        cols = feats // n_img
        class_count = class_exponent.shape[0]
        parts = max(c for c in (6, 3, 2, 1) if rows % (16 * c) == 0 or c == 1)
        dma = pltpu.SemaphoreType.DMA
        vmem = pl.BlockSpec(memory_space=pltpu.VMEM)
        far = pl.BlockSpec(memory_space=pl.ANY)
        new, evidence = pl.pallas_call(
            functools.partial(kernel, n_img, n_tpl, parts),
            out_shape=(
                pltpu.VMEM((tpl_rows, cols), jnp.float32),
                pltpu.VMEM((1, n_tpl * rows), jnp.float32),
            ),
            in_specs=[far, far, pl.BlockSpec(memory_space=pltpu.SMEM), far],
            out_specs=(vmem, vmem),
            scratch_shapes=[
                pltpu.VMEM((tpl_rows, feats), jnp.bfloat16),
                pltpu.VMEM((class_count, n_tpl * rows), jnp.int32),
                dma((3,)),
                pltpu.VMEM((n_tpl, rows, feats), jnp.bfloat16),
                pltpu.VMEM((chips, class_count, 2 * rows), jnp.int32),
                pltpu.VMEM((chips, 1, 2 * rows), jnp.float32),
                pltpu.VMEM((chips, tpl_rows, 2 * rows), jnp.float32),
                pltpu.VMEM((chips, tpl_rows, 2 * rows), jnp.bfloat16),
                pltpu.VMEM((chips, n_tpl, 2, 2 * rows), jnp.float32),
                pltpu.VMEM((tpl_rows, feats), jnp.float32),
                pltpu.VMEM((tpl_rows, cols), jnp.float32),
                pltpu.VMEM((n_img, tpl_rows, cols), jnp.bfloat16),
                pltpu.VMEM((n_img, tpl_rows, cols), jnp.bfloat16),
                pltpu.VMEM((tpl_rows, 1), jnp.float32),
                pltpu.VMEM((tpl_rows, 1), jnp.float32),
                pltpu.VMEM((8, tpl_rows), jnp.float32),
                pltpu.VMEM((n_img, 8, tpl_rows), jnp.float32),
                dma((3, chips, parts)),
                dma((n_tpl, parts)),
                dma((chips, n_tpl)),
                dma((chips, n_tpl)),
                dma((n_img, n_img)),
                dma((n_img, n_img)),
                dma((n_img,)),
                dma((n_img,)),
                pltpu.VMEM((chips, 2, 1, 2 * rows), jnp.float32),
                pltpu.VMEM((2, 1, 2 * rows), jnp.float32),
                pltpu.VMEM((tpl_rows, feats), jnp.bfloat16),
                pltpu.VMEM((tpl_rows, 2 * rows), jnp.float32),
                pltpu.VMEM((tpl_rows, 2 * rows), jnp.bfloat16),
                pltpu.VMEM((tpl_rows, 1), jnp.float32),
                pltpu.VMEM((tpl_rows, 1), jnp.float32),
                pltpu.VMEM((tpl_rows, cols), jnp.float32),
                pltpu.VMEM((n_img, tpl_rows, cols), jnp.bfloat16),
                pltpu.VMEM((n_img, tpl_rows, cols), jnp.bfloat16),
                pltpu.VMEM((tpl_rows, cols), jnp.bfloat16),
                pltpu.VMEM((tpl_rows, cols), jnp.bfloat16),
                pltpu.VMEM((8, tpl_rows), jnp.float32),
                pltpu.VMEM((8, tpl_rows), jnp.float32),
                dma((n_img, 2)),
                dma((n_img, 2)),
                dma((chips, n_tpl)),
                dma((n_img, n_img)),
                dma((n_img, n_img)),
                dma((n_img,)),
                dma((n_img,)),
                dma((2,)),
                dma((2,)),
            ],
            compiler_params=pltpu.CompilerParams(
                collective_id=0, has_side_effects=True, vmem_limit_bytes=60 * 1024 * 1024),
        )(images, templates, class_exponent, class_mask.T)
        return pl.pallas_call(
            emit,
            out_shape=(
                jax.ShapeDtypeStruct(new.shape, jnp.float32),
                jax.ShapeDtypeStruct((n_tpl * rows,), jnp.float32),
            ),
            in_specs=[vmem] * 2,
            out_specs=(far, vmem),
            scratch_shapes=[dma],
        )(*[pltpu.with_memory_space_constraint(x, pltpu.VMEM) for x in (new, evidence)])

    in_specs = (P(("img", "tpl"), None), P("tpl", None), P(), P("img", None))
    out_specs = (P("tpl", "img"), P("img"))
    return jax.shard_map(
        per_device, mesh=mesh, in_specs=in_specs, out_specs=out_specs, check_vma=False
    )
```

```python
import functools

import jax
import jax.numpy as jnp
from jax import lax
from jax.experimental import pallas as pl
from jax.experimental.pallas import tpu as pltpu
from jax.sharding import PartitionSpec as P

MESH = pl.DeviceIdType.MESH
floor_score = -1e30


def kernel(
    n_img, n_tpl, parts, x_ref, t_hbm, power_ref, mask_hbm, out_ref, le_ref,
    t_ref, mask_ref, loads, imgs, allow, le_row, e_ref, post_ref, st, acc, own, sbuf, rbuf, sqn, occ, obuf, orecv,
    img_send, img_recv, st_send, st_recv, rs_send, rs_recv, oc_send, oc_recv,
    here, there, et_ref, e_end, post_end, sqn_end, occ_end, own_end, sbuf_end, rbuf_end, zsend, zrecv, obuf_end, orecv_end,
    et_send, et_recv, est_send, ers_send, ers_recv, z_send, z_recv, hand_send, hand_recv,
):
    chips = n_tpl // 2
    last = chips - 1
    hubs = chips >= 4
    rows, feats = x_ref.shape
    cols = feats // n_img
    me_i, me_t = lax.axis_index("img"), lax.axis_index("tpl")
    chip, core = lax.div(me_t, 2), lax.rem(me_t, 2)
    sibling = 2 * chip + 1 - core
    side = lax.div(2 * chip, chips)
    inward = 1 - 2 * side
    rank = chip + side * (last - 2 * chip)
    inner, outer = me_t + 2 * inward, me_t - 2 * inward
    is_end = jnp.logical_and(rank == 0, hubs)
    is_hub = jnp.logical_and(rank == 1, hubs)
    skip = jnp.where(is_end, 1, 0)
    end_slot = outer
    opposite = last * (1 - side)

    def absent(q, who):
        if not hubs:
            return False
        low = jnp.logical_and(q == 1, who == 0)
        return jnp.logical_or(low, jnp.logical_and(q == last - 1, who == last))

    def tpl_peer(off):
        return lax.rem(me_t + off, n_tpl)

    def img_peer(off):
        return lax.rem(me_i + off, n_img)

    barrier = pltpu.get_barrier_semaphore()
    for off in range(1, n_tpl):
        pl.semaphore_signal(barrier, inc=1, device_id={"tpl": tpl_peer(off)}, device_id_type=MESH)
    for off in range(1, n_img):
        pl.semaphore_signal(barrier, inc=1, device_id={"img": img_peer(off)}, device_id_type=MESH)
    load_t = pltpu.make_async_copy(t_hbm, t_ref, loads.at[0])
    load_x = pltpu.make_async_copy(x_ref, imgs.at[me_t], loads.at[1])
    load_mask = pltpu.make_async_copy(mask_hbm, mask_ref, loads.at[2])
    for load in (load_t, load_x, load_mask):
        load.start()
    pl.semaphore_wait(barrier, n_tpl - 1 + n_img - 1)

    size = rows // parts
    tpl_rows = t_ref.shape[0]
    quarter = tpl_rows // n_img
    t_parts = 2 if quarter % 32 == 0 else 1
    t_size = quarter // t_parts

    pair = 2 * rows
    ahead = 2 * rows // 3
    split = hubs and parts % 3 == 0 and ahead % 128 == 0 and pair == 3 * ahead
    early = ((0, ahead), (pair - ahead, pair)) if split else ()
    late_lanes = ((ahead, pair - ahead),) if split else ((0, pair),)

    def image_copy(src, block, k, way, to):
        place = k + lax.rem(block, 2) * (parts - 1 - 2 * k) if split else k
        piece = pl.ds(pl.multiple_of(place * size, size), size)
        return pltpu.make_async_remote_copy(
            src_ref=src.at[piece], dst_ref=imgs.at[block, piece],
            send_sem=img_send.at[way, lax.div(block, 2), k],
            recv_sem=img_recv.at[block, k], device_id={"tpl": to}, device_id_type=MESH)

    def share_rows(owner, k):
        return pl.ds(owner * quarter + k * t_size, t_size)

    def end_copy(k):
        piece = share_rows(me_i, k)
        return pltpu.make_async_remote_copy(
            src_ref=t_hbm.at[piece], dst_ref=et_ref.at[piece], send_sem=et_send.at[0, k],
            recv_sem=et_recv.at[me_i, k], device_id={"tpl": inner}, device_id_type=MESH)

    def spread_copy(off, k):
        piece = share_rows(me_i, k)
        return pltpu.make_async_remote_copy(
            src_ref=et_ref.at[piece], dst_ref=et_ref.at[piece], send_sem=et_send.at[off, k],
            recv_sem=et_recv.at[me_i, k], device_id={"img": flip(off)}, device_id_type=MESH)

    def end_arrival(owner, k):
        piece = share_rows(owner, k)
        return pltpu.make_async_remote_copy(
            src_ref=et_ref.at[piece], dst_ref=et_ref.at[piece], send_sem=et_send.at[0, k],
            recv_sem=et_recv.at[owner, k], device_id={"img": img_peer(1)}, device_id_type=MESH)

    own_block = 2 * chip + core
    sends_out = jnp.logical_and(rank > 0, jnp.logical_not(is_hub))
    if hubs:
        @pl.when(is_end)
        def _():
            for k in range(t_parts):
                end_copy(k).start()

    for k in range(parts):
        if chips > 1:
            image_copy(x_ref, own_block, k, 0, inner).start()

        @pl.when(sends_out)
        def _():
            image_copy(x_ref, own_block, k, 1, outer).start()

        image_copy(x_ref, own_block, k, 2, sibling).start()

    for load in (load_t, load_x, load_mask):
        load.wait()

    def half_norm(ref):
        tf = ref[...].astype(jnp.float32)
        return 0.5 * jnp.sum(tf * tf, axis=1, keepdims=True)

    sqn[...] = half_norm(t_ref)
    acc[...] = jnp.zeros_like(acc)
    occ[...] = jnp.zeros_like(occ)

    def stat_copy(q, slot, off, sems):
        return pltpu.make_async_remote_copy(
            src_ref=st.at[q, slot], dst_ref=st.at[q, slot], send_sem=sems.at[q, off],
            recv_sem=st_recv.at[q, slot], device_id={"tpl": tpl_peer(off)}, device_id_type=MESH)

    def stat_arrival(q, slot):
        return pltpu.make_async_remote_copy(
            src_ref=st.at[q, slot], dst_ref=st.at[q, slot], send_sem=st_send.at[q, 0],
            recv_sem=st_recv.at[q, slot], device_id={"tpl": tpl_peer(1)}, device_id_type=MESH)

    def tell(q, slot, sems):
        for off in sorted(range(1, n_tpl), key=lambda o: abs(o - n_tpl // 2)):
            @pl.when(jnp.logical_not(absent(q, lax.div(tpl_peer(off), 2))))
            def _():
                stat_copy(q, slot, off, sems).start()

    def told(q, slot, sems):
        for off in range(1, n_tpl):
            @pl.when(jnp.logical_not(absent(q, lax.div(tpl_peer(off), 2))))
            def _():
                stat_copy(q, slot, off, sems).wait_send()

    def pair_of(q):
        return imgs[pl.ds(2 * q, 2)].reshape(2 * rows, feats)

    def images_of(q, lanes):
        cuts = [(c, max(lo - c * rows, 0), min(hi - c * rows, rows)) for lo, hi in lanes for c in range(2)]
        return jnp.concatenate([imgs[2 * q + c, lo:hi] for c, lo, hi in cuts if lo < hi])

    class_count = power_ref.shape[0]
    per_class = tpl_rows * n_tpl // class_count
    for q in range(chips):
        allow[q] = mask_ref[:, q * pair:(q + 1) * pair]

    def inverse_temp(c):
        power = jnp.full((1, pair), power_ref[c], jnp.int32)
        return 0.5 * jnp.exp2(0.5 * power.astype(jnp.float32))

    def class_terms(slot, q, lanes):
        first = slot * tpl_rows
        width = sum(hi - lo for lo, hi in lanes)

        def mask_of(c):
            row = allow[q, pl.ds(c, 1), :]
            return jnp.concatenate([row[:, lo:hi] for lo, hi in lanes], axis=1)

        if per_class % tpl_rows == 0:
            only = lax.div(first, per_class)
            return inverse_temp(only)[:, :width], mask_of(only) > 0
        owner = lax.div(first + lax.broadcasted_iota(jnp.int32, (tpl_rows, width), 0), per_class)
        beta = sum(jnp.where(owner == c, inverse_temp(c)[:, :width], 0.0) for c in range(class_count))
        return beta, sum(jnp.where(owner == c, mask_of(c), 0) for c in range(class_count)) > 0

    def score(q, slot, tpl, norm, e_out, tops, totals, lanes=None):
        images = pair_of(q) if lanes is None else images_of(q, lanes)
        lanes = lanes or ((0, pair),)
        raw = lax.dot_general(
            tpl[...], images, (((1,), (1,)), ((), ())), preferred_element_type=jnp.float32)
        beta, allowed = class_terms(slot, q, lanes)
        s = beta * (raw - norm[...])
        top = jnp.max(jnp.where(allowed, s, floor_score), axis=0, keepdims=True)
        e = jnp.where(allowed, jnp.exp(s - top), 0.0)
        total = jnp.sum(e, axis=0, keepdims=True)
        at = 0
        for lo, hi in lanes:
            tops[:, lo:hi] = top[:, at:at + hi - lo]
            totals[:, lo:hi] = total[:, at:at + hi - lo]
            if e_out is not None:
                e_out[:, lo:hi] = e[:, at:at + hi - lo]
            at += hi - lo

    def own_score(q, lanes=None):
        score(q, me_t, t_ref, sqn, e_ref.at[q], here.at[q, 0], here.at[q, 1], lanes)

    def end_score(q, lanes=None):
        score(q, end_slot, et_ref, sqn_end, e_end if q is chip else None, there.at[0], there.at[1], lanes)

    def put_stats(q):
        st[q, me_t, 0:1, :] = here[q, 0]
        st[q, me_t, 1:2, :] = here[q, 1]

    def put_joint_stats(q):
        top = jnp.maximum(here[q, 0], there[0])
        st[q, me_t, 0:1, :] = top
        st[q, me_t, 1:2, :] = here[q, 1] * jnp.exp(here[q, 0] - top) + there[1] * jnp.exp(there[0] - top)

    def wait_image(block, k):
        image_copy(imgs.at[block], block, k, 2, sibling).wait_recv()

    def relay(q, k, more, way, to):
        block = 2 * q + core
        wait_image(block, k)

        @pl.when(more)
        def _():
            image_copy(imgs.at[block], block, k, way, to).start()

        image_copy(imgs.at[block], block, k, 2, sibling).start()

    def wait_sibling(q):
        for k in range(parts):
            wait_image(2 * q + 1 - core, k)

    def finish(q):
        wait_sibling(q)
        own_score(q)
        put_stats(q)
        tell(q, me_t, st_send)

    def ready(k):
        return k == 2 * parts // 3

    def finish_ahead(q):
        for k in range(2 * parts // 3):
            wait_image(2 * q + 1 - core, k)
        own_score(q, early)

        @pl.when(is_hub)
        def _():
            end_score(q, early)

    def finish_last(q):
        for k in range(2 * parts // 3 if split else 0, parts):
            wait_image(2 * q + 1 - core, k)
        own_score(q, late_lanes)

        @pl.when(is_hub)
        def _():
            end_score(q, late_lanes)
            put_joint_stats(q)
            tell(q, me_t, st_send)

    def mute(q, who):
        if not hubs:
            return False
        low = jnp.logical_and(q == last, who == 0)
        return jnp.logical_or(low, jnp.logical_and(q == 0, who == last))

    def gather_stats(q):
        for off in range(1, n_tpl):
            slot = tpl_peer(off)
            silent = jnp.logical_or(is_hub & (q == chip) & (slot == end_slot), mute(q, lax.div(slot, 2)))

            @pl.when(jnp.logical_not(silent))
            def _():
                stat_arrival(q, slot).wait_recv()

        heard = range(n_tpl)
        if hubs and isinstance(q, int):
            heard = [j for j in heard if not (q == last and j < 2) and not (q == 0 and j >= 2 * last)]
        tops = {j: st[q, j, 0:1, :] for j in heard}
        top = functools.reduce(jnp.maximum, tops.values())
        total = sum(st[q, j, 1:2, :] * jnp.exp(tops[j] - top) for j in heard)
        le_row[q] = top + jnp.log(total)
        return top, total

    def weigh(e, local, top, total):
        return e[...] * (jnp.exp(local - top) / total)

    def consume(q, count=True):
        top, total = gather_stats(q)
        post = weigh(e_ref.at[q], here[q, 0], top, total)
        post_ref[q] = post.astype(jnp.bfloat16)
        if count:
            occ[...] += jnp.sum(post, axis=1, keepdims=True)
        else:
            e_ref[q] = post
        return top, total

    bits = [1 << k for k in range(n_img.bit_length() - 1)]
    groups = len(bits) if bits and tpl_rows % (16 * len(bits)) == 0 else 1
    depth = tpl_rows // groups
    orders = [bits[g:] + bits[:g] for g in range(groups)]
    masks = sorted(range(1, n_img), key=lambda mask: -mask.bit_count())

    def flip(mask):
        return me_i + sum(b - 2 * b * lax.rem(lax.div(me_i, b), 2) for b in bits if b & mask)

    def turn(g, mask):
        return next(r for r, b in enumerate(orders[g]) if b & mask)

    def band(g):
        return slice(g * depth, (g + 1) * depth)

    def part_of(mask):
        return pl.ds(pl.multiple_of(flip(mask) * cols, cols), cols)

    class Reduction:
        def __init__(self, src, dst, sent, got, share):
            self.src, self.dst, self.sent, self.got, self.share = src, dst, sent, got, share

        def copy(self, g, mask):
            return pltpu.make_async_remote_copy(
                src_ref=self.src.at[mask, band(g)], dst_ref=self.dst.at[mask, band(g)],
                send_sem=self.sent.at[g, mask], recv_sem=self.got.at[g, mask],
                device_id={"img": flip(orders[g][turn(g, mask)])}, device_id_type=MESH)

        def received(self, g, mask, rounds):
            value = 0.0
            for b in orders[g][:rounds]:
                self.copy(g, b + mask).wait_recv()
                value += self.dst[b + mask, band(g)].astype(jnp.float32)
            return value

        def round(self, r):
            for mask in masks:
                for g in range(groups):
                    if turn(g, mask) == r:
                        value = self.share(g, mask)
                        self.src[mask, band(g)] = (value + self.received(g, mask, r)).astype(jnp.bfloat16)
                        self.copy(g, mask).start()

        def drain(self):
            for mask in masks:
                for g in range(groups):
                    self.copy(g, mask).wait_send()

    def share_end(g, mask):
        block = imgs[pl.ds(2 * chip, 2), :, part_of(mask)].reshape(2 * rows, cols)
        return jnp.dot(post_end[band(g)], block, preferred_element_type=jnp.float32)

    reduce_end = Reduction(sbuf_end, rbuf_end, ers_send, ers_recv, share_end)

    def row_of(column):
        return jnp.transpose(jnp.broadcast_to(column, (tpl_rows, 128)))[0:8]

    def hand_occ():
        return pltpu.make_async_remote_copy(
            src_ref=obuf_end, dst_ref=orecv_end, send_sem=hand_send.at[0],
            recv_sem=hand_recv.at[0], device_id={"tpl": outer}, device_id_type=MESH)

    def hand_evidence(q):
        return pltpu.make_async_remote_copy(
            src_ref=le_row.at[q], dst_ref=le_row.at[q], send_sem=hand_send.at[1],
            recv_sem=hand_recv.at[1], device_id={"tpl": outer}, device_id_type=MESH)

    def hand_sum(g):
        return pltpu.make_async_remote_copy(
            src_ref=zsend.at[band(g)], dst_ref=zrecv.at[band(g)], send_sem=z_send.at[g],
            recv_sem=z_recv.at[g], device_id={"tpl": outer}, device_id_type=MESH)

    def hub_spread(k):
        end_arrival(me_i, k).wait_recv()
        for off in masks:
            spread_copy(off, k).start()

    def hub_score():
        for off in range(1, n_img):
            for k in range(t_parts):
                end_arrival(img_peer(off), k).wait_recv()
        sqn_end[...] = half_norm(et_ref)
        end_score(chip)
        st[chip, end_slot, 0:1, :] = there[0]
        st[chip, end_slot, 1:2, :] = there[1]
        tell(chip, end_slot, est_send)

    def hub_consume():
        top, total = consume(chip)
        post = weigh(e_end, there[0], top, total)
        obuf_end[...] = row_of(jnp.sum(post, axis=1, keepdims=True))
        post_end[...] = post.astype(jnp.bfloat16)
        reduce_end.round(0)
        hand_occ().start()
        hand_evidence(chip).start()

    def middle(q, carry):
        @pl.when(jnp.logical_not(jnp.logical_or(absent(q, chip), is_hub & (q == chip))))
        def _():
            consume(q)

        @pl.when(jnp.logical_not(absent(q, chip)))
        def _():
            for j in range(n_img):
                part = slice(j * cols, (j + 1) * cols)
                block = imgs[pl.ds(2 * q, 2), :, part].reshape(2 * rows, cols)
                acc[:, part] += jnp.dot(post_ref[q], block, preferred_element_type=jnp.float32)

        return carry

    def middles():
        lax.fori_loop(1, chips - 1, middle, 0)

    finish(chip)
    n_far = last - rank - skip
    late = parts // 2 if hubs else 0

    def arrive(b, carry):
        q_far = chip + inward * (b + 1 + skip)

        def near_event(block, k):
            q_near = chip - inward * (block + 1)
            there = jnp.logical_and(block >= 0, block < rank)

            @pl.when(there)
            def _():
                relay(q_near, k, last > 0, 0, inner)

            if k == parts - 1:
                @pl.when(there)
                def _():
                    finish(q_near)

        for k in range(parts):
            @pl.when(b < n_far)
            def _():
                relay(q_far, k, rank > 0, 1, outer)

            if split and ready(k):
                @pl.when(jnp.logical_or(is_end, is_hub) & (b < n_far) & (q_far == opposite))
                def _():
                    finish_ahead(q_far)

            if k >= late:
                near_event(b, k - late)
            else:
                near_event(b - 1, k - late + parts)
            if hubs:
                spreads = [j for j in range(t_parts) if k == min(2 * j, parts - 1)]
                if spreads:
                    @pl.when(jnp.logical_and(is_hub, b == 0))
                    def _():
                        for j in spreads:
                            hub_spread(j)

                if k == parts // 2:
                    @pl.when(jnp.logical_and(is_end, b == n_far - 1))
                    def _():
                        middles()

                steps = ((parts // 3 - 1, hub_score), (parts // 2, hub_consume))
                due = [step for at, step in steps if k == max(0, min(at, parts - 1))]
                if due:
                    @pl.when(jnp.logical_and(is_hub, b == 1))
                    def _():
                        for step in due:
                            step()

        speaks = jnp.logical_or(is_end, is_hub) & (q_far == opposite)

        @pl.when(jnp.logical_and(b < n_far, jnp.logical_not(speaks)))
        def _():
            finish(q_far)

        if hubs:
            @pl.when(jnp.logical_and(b < n_far, speaks))
            def _():
                finish_last(q_far)

        return carry

    lax.fori_loop(0, last - 1 if hubs else last, arrive, 0)

    if hubs:
        @pl.when(is_hub)
        def _():
            for r in range(1, len(bits)):
                reduce_end.round(r)
            for g in range(groups):
                own_end[band(g)] = share_end(g, 0)

    @pl.when(jnp.logical_not(is_end))
    def _():
        middles()

    ends = (0, chips - 1) if chips > 1 else (0,)
    for q in ends:
        consume(q, count=False)

    def occ_copy(off):
        return pltpu.make_async_remote_copy(
            src_ref=obuf, dst_ref=orecv.at[off], send_sem=oc_send.at[off],
            recv_sem=oc_recv.at[off], device_id={"img": img_peer(off)}, device_id_type=MESH)

    def share(g, mask):
        part = part_of(mask)
        value = acc[band(g), part]
        for q in ends:
            block = imgs[2 * q:2 * q + 2, :, part].reshape(2 * rows, cols)
            value += jnp.dot(post_ref[q, band(g)], block, preferred_element_type=jnp.float32)
        return value

    reduce_own = Reduction(sbuf, rbuf, rs_send, rs_recv, share)
    mine = part_of(0)
    for r in range(len(bits)):
        reduce_own.round(r)
        if r == 0:
            for q in ends:
                occ[...] += jnp.sum(e_ref[q], axis=1, keepdims=True)
            obuf[...] = row_of(occ[...])
            if hubs:
                @pl.when(is_end)
                def _():
                    hand_occ().wait_recv()
                    hand_evidence(chip + inward).wait_recv()
                    obuf[...] += orecv_end[...]

            for off in range(1, n_img):
                occ_copy(off).start()
            for q in range(chips):
                le_ref[:, q * pair:(q + 1) * pair] = le_row[q]
            if hubs:
                @pl.when(is_hub)
                def _():
                    for g in range(groups):
                        zsend[band(g)] = (own_end[band(g)] + reduce_end.received(g, 0, len(bits))).astype(jnp.bfloat16)
                        hand_sum(g).start()

            for g in range(groups):
                own[band(g)] = share(g, 0) + t_ref[band(g), mine].astype(jnp.float32)
    if hubs:
        @pl.when(is_end)
        def _():
            for k in range(t_parts):
                end_copy(k).wait_send()

        @pl.when(is_hub)
        def _():
            for off in range(1, n_img):
                for k in range(t_parts):
                    spread_copy(off, k).wait_send()
            told(chip, end_slot, est_send)
            hand_occ().wait_send()
            hand_evidence(chip).wait_send()
            reduce_end.drain()

    def drain(q, carry):
        block = 2 * q + core
        away = (q - chip) * inward
        goes_out = (rank > 0) & (away >= 0) & jnp.logical_not(is_hub & (away == 0))
        for k in range(parts):
            @pl.when((away <= 0) & (last > 0))
            def _():
                image_copy(imgs.at[block], block, k, 0, inner).wait_send()

            @pl.when(goes_out)
            def _():
                image_copy(imgs.at[block], block, k, 1, outer).wait_send()

            @pl.when(jnp.logical_not(absent(q, chip)))
            def _():
                image_copy(imgs.at[block], block, k, 2, sibling).wait_send()

        @pl.when(jnp.logical_not(jnp.logical_or(absent(q, chip), is_end & (q == opposite))))
        def _():
            told(q, me_t, st_send)

        return carry

    lax.fori_loop(0, chips, drain, 0)

    occ_row = obuf[...]
    for off in range(1, n_img):
        occ_copy(off).wait_recv()
        occ_row += orecv[off]
    occ_col = jnp.transpose(jnp.broadcast_to(occ_row[0:1], (128, tpl_rows)))[:, 0:1]
    occ[...] = occ_col + 1.0

    if hubs:
        @pl.when(is_end)
        def _():
            for g in range(groups):
                hand_sum(g).wait_recv()
                own[band(g)] += zrecv[band(g)].astype(jnp.float32)

    for g in range(groups):
        out_ref[band(g)] = (own[band(g)] + reduce_own.received(g, 0, len(bits))) / occ[band(g)]

    for off in range(1, n_img):
        occ_copy(off).wait_send()
    reduce_own.drain()
    if hubs:
        @pl.when(is_hub)
        def _():
            for g in range(groups):
                hand_sum(g).wait_send()


def emit(new_ref, evidence_ref, new_out, evidence_out, sem):
    move = pltpu.make_async_copy(new_ref, new_out, sem)
    move.start()
    evidence_out[...] = evidence_ref[...].reshape(evidence_out.shape)
    move.wait()


def solution(mesh):
    n_img, n_tpl = mesh.shape["img"], mesh.shape["tpl"]
    chips = n_tpl // 2

    def per_device(images, templates, class_exponent, class_mask):
        rows, feats = images.shape
        tpl_rows = templates.shape[0]
        cols = feats // n_img
        class_count = class_exponent.shape[0]
        parts = max(c for c in (6, 3, 2, 1) if rows % (16 * c) == 0 or c == 1)
        dma = pltpu.SemaphoreType.DMA
        vmem = pl.BlockSpec(memory_space=pltpu.VMEM)
        far = pl.BlockSpec(memory_space=pl.ANY)
        new, evidence = pl.pallas_call(
            functools.partial(kernel, n_img, n_tpl, parts),
            out_shape=(
                pltpu.VMEM((tpl_rows, cols), jnp.float32),
                pltpu.VMEM((1, n_tpl * rows), jnp.float32),
            ),
            in_specs=[far, far, pl.BlockSpec(memory_space=pltpu.SMEM), far],
            out_specs=(vmem, vmem),
            scratch_shapes=[
                pltpu.VMEM((tpl_rows, feats), jnp.bfloat16),
                pltpu.VMEM((class_count, n_tpl * rows), jnp.int32),
                dma((3,)),
                pltpu.VMEM((n_tpl, rows, feats), jnp.bfloat16),
                pltpu.VMEM((chips, class_count, 2 * rows), jnp.int32),
                pltpu.VMEM((chips, 1, 2 * rows), jnp.float32),
                pltpu.VMEM((chips, tpl_rows, 2 * rows), jnp.float32),
                pltpu.VMEM((chips, tpl_rows, 2 * rows), jnp.bfloat16),
                pltpu.VMEM((chips, n_tpl, 2, 2 * rows), jnp.float32),
                pltpu.VMEM((tpl_rows, feats), jnp.float32),
                pltpu.VMEM((tpl_rows, cols), jnp.float32),
                pltpu.VMEM((n_img, tpl_rows, cols), jnp.bfloat16),
                pltpu.VMEM((n_img, tpl_rows, cols), jnp.bfloat16),
                pltpu.VMEM((tpl_rows, 1), jnp.float32),
                pltpu.VMEM((tpl_rows, 1), jnp.float32),
                pltpu.VMEM((8, tpl_rows), jnp.float32),
                pltpu.VMEM((n_img, 8, tpl_rows), jnp.float32),
                dma((3, chips, parts)),
                dma((n_tpl, parts)),
                dma((chips, n_tpl)),
                dma((chips, n_tpl)),
                dma((n_img, n_img)),
                dma((n_img, n_img)),
                dma((n_img,)),
                dma((n_img,)),
                pltpu.VMEM((chips, 2, 1, 2 * rows), jnp.float32),
                pltpu.VMEM((2, 1, 2 * rows), jnp.float32),
                pltpu.VMEM((tpl_rows, feats), jnp.bfloat16),
                pltpu.VMEM((tpl_rows, 2 * rows), jnp.float32),
                pltpu.VMEM((tpl_rows, 2 * rows), jnp.bfloat16),
                pltpu.VMEM((tpl_rows, 1), jnp.float32),
                pltpu.VMEM((tpl_rows, 1), jnp.float32),
                pltpu.VMEM((tpl_rows, cols), jnp.float32),
                pltpu.VMEM((n_img, tpl_rows, cols), jnp.bfloat16),
                pltpu.VMEM((n_img, tpl_rows, cols), jnp.bfloat16),
                pltpu.VMEM((tpl_rows, cols), jnp.bfloat16),
                pltpu.VMEM((tpl_rows, cols), jnp.bfloat16),
                pltpu.VMEM((8, tpl_rows), jnp.float32),
                pltpu.VMEM((8, tpl_rows), jnp.float32),
                dma((n_img, 2)),
                dma((n_img, 2)),
                dma((chips, n_tpl)),
                dma((n_img, n_img)),
                dma((n_img, n_img)),
                dma((n_img,)),
                dma((n_img,)),
                dma((2,)),
                dma((2,)),
            ],
            compiler_params=pltpu.CompilerParams(
                collective_id=0, has_side_effects=True, vmem_limit_bytes=60 * 1024 * 1024),
        )(images, templates, class_exponent, class_mask.T)
        return pl.pallas_call(
            emit,
            out_shape=(
                jax.ShapeDtypeStruct(new.shape, jnp.float32),
                jax.ShapeDtypeStruct((n_tpl * rows,), jnp.float32),
            ),
            in_specs=[vmem] * 2,
            out_specs=(far, vmem),
            scratch_shapes=[dma],
        )(*[pltpu.with_memory_space_constraint(x, pltpu.VMEM) for x in (new, evidence)])

    in_specs = (P(("img", "tpl"), None), P("tpl", None), P(), P("img", None))
    out_specs = (P("tpl", "img"), P("img"))
    return jax.shard_map(
        per_device, mesh=mesh, in_specs=in_specs, out_specs=out_specs, check_vma=False
    )
```

```python
import functools

import jax
import jax.numpy as jnp
from jax import lax
from jax.experimental import pallas as pl
from jax.experimental.pallas import tpu as pltpu
from jax.sharding import PartitionSpec as P

MESH = pl.DeviceIdType.MESH
floor_score = -1e30


def kernel(
    n_img, n_tpl, parts, x_ref, t_hbm, power_ref, mask_hbm, out_ref, le_ref,
    t_ref, mask_ref, loads, imgs, allow, le_row, e_ref, post_ref, st, acc, own, sbuf, rbuf, sqn, occ, obuf, orecv,
    img_send, img_recv, st_send, st_recv, rs_send, rs_recv, oc_send, oc_recv,
    here, there, et_ref, e_end, post_end, sqn_end, occ_end, own_end, sbuf_end, rbuf_end, zsend, zrecv, obuf_end, orecv_end,
    et_send, et_recv, est_send, ers_send, ers_recv, z_send, z_recv, hand_send, hand_recv,
):
    chips = n_tpl // 2
    last = chips - 1
    hubs = chips >= 4
    rows, feats = x_ref.shape
    cols = feats // n_img
    me_i, me_t = lax.axis_index("img"), lax.axis_index("tpl")
    chip, core = lax.div(me_t, 2), lax.rem(me_t, 2)
    sibling = 2 * chip + 1 - core
    side = lax.div(2 * chip, chips)
    inward = 1 - 2 * side
    rank = chip + side * (last - 2 * chip)
    inner, outer = me_t + 2 * inward, me_t - 2 * inward
    is_end = jnp.logical_and(rank == 0, hubs)
    is_hub = jnp.logical_and(rank == 1, hubs)
    skip = jnp.where(is_end, 1, 0)
    end_slot = outer
    opposite = last * (1 - side)

    def absent(q, who):
        if not hubs:
            return False
        low = jnp.logical_and(q == 1, who == 0)
        return jnp.logical_or(low, jnp.logical_and(q == last - 1, who == last))

    def tpl_peer(off):
        return lax.rem(me_t + off, n_tpl)

    def img_peer(off):
        return lax.rem(me_i + off, n_img)

    barrier = pltpu.get_barrier_semaphore()
    for off in range(1, n_tpl):
        pl.semaphore_signal(barrier, inc=1, device_id={"tpl": tpl_peer(off)}, device_id_type=MESH)
    for off in range(1, n_img):
        pl.semaphore_signal(barrier, inc=1, device_id={"img": img_peer(off)}, device_id_type=MESH)
    load_t = pltpu.make_async_copy(t_hbm, t_ref, loads.at[0])
    load_x = pltpu.make_async_copy(x_ref, imgs.at[me_t], loads.at[1])
    load_mask = pltpu.make_async_copy(mask_hbm, mask_ref, loads.at[2])
    for load in (load_t, load_x, load_mask):
        load.start()
    pl.semaphore_wait(barrier, n_tpl - 1 + n_img - 1)

    size = rows // parts
    tpl_rows = t_ref.shape[0]
    quarter = tpl_rows // n_img
    t_parts = 2 if quarter % 32 == 0 else 1
    t_size = quarter // t_parts

    pair = 2 * rows
    ahead = 2 * rows // 3
    split = hubs and parts % 3 == 0 and ahead % 128 == 0 and pair == 3 * ahead
    early = ((0, ahead), (pair - ahead, pair)) if split else ()
    late_lanes = ((ahead, pair - ahead),) if split else ((0, pair),)

    def image_copy(src, block, k, way, to):
        place = k + lax.rem(block, 2) * (parts - 1 - 2 * k) if split else k
        piece = pl.ds(pl.multiple_of(place * size, size), size)
        return pltpu.make_async_remote_copy(
            src_ref=src.at[piece], dst_ref=imgs.at[block, piece],
            send_sem=img_send.at[way, lax.div(block, 2), k],
            recv_sem=img_recv.at[block, k], device_id={"tpl": to}, device_id_type=MESH)

    def share_rows(owner, k):
        return pl.ds(owner * quarter + k * t_size, t_size)

    def end_copy(k):
        piece = share_rows(me_i, k)
        return pltpu.make_async_remote_copy(
            src_ref=t_hbm.at[piece], dst_ref=et_ref.at[piece], send_sem=et_send.at[0, k],
            recv_sem=et_recv.at[me_i, k], device_id={"tpl": inner}, device_id_type=MESH)

    def spread_copy(off, k):
        piece = share_rows(me_i, k)
        return pltpu.make_async_remote_copy(
            src_ref=et_ref.at[piece], dst_ref=et_ref.at[piece], send_sem=et_send.at[off, k],
            recv_sem=et_recv.at[me_i, k], device_id={"img": flip(off)}, device_id_type=MESH)

    def end_arrival(owner, k):
        piece = share_rows(owner, k)
        return pltpu.make_async_remote_copy(
            src_ref=et_ref.at[piece], dst_ref=et_ref.at[piece], send_sem=et_send.at[0, k],
            recv_sem=et_recv.at[owner, k], device_id={"img": img_peer(1)}, device_id_type=MESH)

    own_block = 2 * chip + core
    sends_out = jnp.logical_and(rank > 0, jnp.logical_not(is_hub))
    if hubs:
        @pl.when(is_end)
        def _():
            for k in range(t_parts):
                end_copy(k).start()

    for k in range(parts):
        if chips > 1:
            image_copy(x_ref, own_block, k, 0, inner).start()

        @pl.when(sends_out)
        def _():
            image_copy(x_ref, own_block, k, 1, outer).start()

        image_copy(x_ref, own_block, k, 2, sibling).start()

    for load in (load_t, load_x, load_mask):
        load.wait()

    def half_norm(ref):
        tf = ref[...].astype(jnp.float32)
        return 0.5 * jnp.sum(tf * tf, axis=1, keepdims=True)

    sqn[...] = half_norm(t_ref)
    acc[...] = jnp.zeros_like(acc)
    occ[...] = jnp.zeros_like(occ)

    def stat_copy(q, slot, off, sems):
        return pltpu.make_async_remote_copy(
            src_ref=st.at[q, slot], dst_ref=st.at[q, slot], send_sem=sems.at[q, off],
            recv_sem=st_recv.at[q, slot], device_id={"tpl": tpl_peer(off)}, device_id_type=MESH)

    def stat_arrival(q, slot):
        return pltpu.make_async_remote_copy(
            src_ref=st.at[q, slot], dst_ref=st.at[q, slot], send_sem=st_send.at[q, 0],
            recv_sem=st_recv.at[q, slot], device_id={"tpl": tpl_peer(1)}, device_id_type=MESH)

    def tell(q, slot, sems):
        for off in sorted(range(1, n_tpl), key=lambda o: abs(o - n_tpl // 2)):
            @pl.when(jnp.logical_not(absent(q, lax.div(tpl_peer(off), 2))))
            def _():
                stat_copy(q, slot, off, sems).start()

    def told(q, slot, sems):
        for off in range(1, n_tpl):
            @pl.when(jnp.logical_not(absent(q, lax.div(tpl_peer(off), 2))))
            def _():
                stat_copy(q, slot, off, sems).wait_send()

    def pair_of(q):
        return imgs[pl.ds(2 * q, 2)].reshape(2 * rows, feats)

    def images_of(q, lanes):
        cuts = [(c, max(lo - c * rows, 0), min(hi - c * rows, rows)) for lo, hi in lanes for c in range(2)]
        return jnp.concatenate([imgs[2 * q + c, lo:hi] for c, lo, hi in cuts if lo < hi])

    class_count = power_ref.shape[0]
    per_class = tpl_rows * n_tpl // class_count
    for q in range(chips):
        allow[q] = mask_ref[:, q * pair:(q + 1) * pair]

    def inverse_temp(c):
        power = jnp.full((1, pair), power_ref[c], jnp.int32)
        return 0.5 * jnp.exp2(0.5 * power.astype(jnp.float32))

    def class_terms(slot, q, lanes):
        first = slot * tpl_rows
        width = sum(hi - lo for lo, hi in lanes)

        def mask_of(c):
            row = allow[q, pl.ds(c, 1), :]
            return jnp.concatenate([row[:, lo:hi] for lo, hi in lanes], axis=1)

        if per_class % tpl_rows == 0:
            only = lax.div(first, per_class)
            return inverse_temp(only)[:, :width], mask_of(only) > 0
        owner = lax.div(first + lax.broadcasted_iota(jnp.int32, (tpl_rows, width), 0), per_class)
        beta = sum(jnp.where(owner == c, inverse_temp(c)[:, :width], 0.0) for c in range(class_count))
        return beta, sum(jnp.where(owner == c, mask_of(c), 0) for c in range(class_count)) > 0

    def score(q, slot, tpl, norm, e_out, tops, totals, lanes=None):
        images = pair_of(q) if lanes is None else images_of(q, lanes)
        lanes = lanes or ((0, pair),)
        raw = lax.dot_general(
            tpl[...], images, (((1,), (1,)), ((), ())), preferred_element_type=jnp.float32)
        beta, allowed = class_terms(slot, q, lanes)
        s = beta * (raw - norm[...])
        top = jnp.max(jnp.where(allowed, s, floor_score), axis=0, keepdims=True)
        e = jnp.where(allowed, jnp.exp(s - top), 0.0)
        total = jnp.sum(e, axis=0, keepdims=True)
        at = 0
        for lo, hi in lanes:
            tops[:, lo:hi] = top[:, at:at + hi - lo]
            totals[:, lo:hi] = total[:, at:at + hi - lo]
            if e_out is not None:
                e_out[:, lo:hi] = e[:, at:at + hi - lo]
            at += hi - lo

    def own_score(q, lanes=None):
        score(q, me_t, t_ref, sqn, e_ref.at[q], here.at[q, 0], here.at[q, 1], lanes)

    def end_score(q, lanes=None):
        score(q, end_slot, et_ref, sqn_end, e_end if q is chip else None, there.at[0], there.at[1], lanes)

    def put_stats(q):
        st[q, me_t, 0:1, :] = here[q, 0]
        st[q, me_t, 1:2, :] = here[q, 1]

    def put_joint_stats(q):
        top = jnp.maximum(here[q, 0], there[0])
        st[q, me_t, 0:1, :] = top
        st[q, me_t, 1:2, :] = here[q, 1] * jnp.exp(here[q, 0] - top) + there[1] * jnp.exp(there[0] - top)

    def wait_image(block, k):
        image_copy(imgs.at[block], block, k, 2, sibling).wait_recv()

    def relay(q, k, more, way, to):
        block = 2 * q + core
        wait_image(block, k)

        @pl.when(more)
        def _():
            image_copy(imgs.at[block], block, k, way, to).start()

        image_copy(imgs.at[block], block, k, 2, sibling).start()

    def wait_sibling(q):
        for k in range(parts):
            wait_image(2 * q + 1 - core, k)

    def finish(q):
        wait_sibling(q)
        own_score(q)
        put_stats(q)
        tell(q, me_t, st_send)

    def ready(k):
        return k == 2 * parts // 3

    def finish_ahead(q):
        for k in range(2 * parts // 3):
            wait_image(2 * q + 1 - core, k)
        own_score(q, early)

        @pl.when(is_hub)
        def _():
            end_score(q, early)

    def finish_last(q):
        for k in range(2 * parts // 3 if split else 0, parts):
            wait_image(2 * q + 1 - core, k)
        own_score(q, late_lanes)

        @pl.when(is_hub)
        def _():
            end_score(q, late_lanes)
            put_joint_stats(q)
            tell(q, me_t, st_send)

    def mute(q, who):
        if not hubs:
            return False
        low = jnp.logical_and(q == last, who == 0)
        return jnp.logical_or(low, jnp.logical_and(q == 0, who == last))

    def gather_stats(q):
        for off in range(1, n_tpl):
            slot = tpl_peer(off)
            silent = jnp.logical_or(is_hub & (q == chip) & (slot == end_slot), mute(q, lax.div(slot, 2)))

            @pl.when(jnp.logical_not(silent))
            def _():
                stat_arrival(q, slot).wait_recv()

        heard = range(n_tpl)
        if hubs and isinstance(q, int):
            heard = [j for j in heard if not (q == last and j < 2) and not (q == 0 and j >= 2 * last)]
        tops = {j: st[q, j, 0:1, :] for j in heard}
        top = functools.reduce(jnp.maximum, tops.values())
        total = sum(st[q, j, 1:2, :] * jnp.exp(tops[j] - top) for j in heard)
        le_row[q] = top + jnp.log(total)
        return top, total

    def weigh(e, local, top, total):
        return e[...] * (jnp.exp(local - top) / total)

    def consume(q):
        top, total = gather_stats(q)
        post = weigh(e_ref.at[q], here[q, 0], top, total)
        post_ref[q] = post.astype(jnp.bfloat16)
        occ[...] += jnp.sum(post, axis=1, keepdims=True)
        return top, total

    bits = [1 << k for k in range(n_img.bit_length() - 1)]
    groups = len(bits) if bits and tpl_rows % (16 * len(bits)) == 0 else 1
    depth = tpl_rows // groups
    orders = [bits[g:] + bits[:g] for g in range(groups)]
    masks = sorted(range(1, n_img), key=lambda mask: -mask.bit_count())

    def flip(mask):
        return me_i + sum(b - 2 * b * lax.rem(lax.div(me_i, b), 2) for b in bits if b & mask)

    def turn(g, mask):
        return next(r for r, b in enumerate(orders[g]) if b & mask)

    def band(g):
        return slice(g * depth, (g + 1) * depth)

    def part_of(mask):
        return pl.ds(pl.multiple_of(flip(mask) * cols, cols), cols)

    class Reduction:
        def __init__(self, src, dst, sent, got, share):
            self.src, self.dst, self.sent, self.got, self.share = src, dst, sent, got, share

        def copy(self, g, mask):
            return pltpu.make_async_remote_copy(
                src_ref=self.src.at[mask, band(g)], dst_ref=self.dst.at[mask, band(g)],
                send_sem=self.sent.at[g, mask], recv_sem=self.got.at[g, mask],
                device_id={"img": flip(orders[g][turn(g, mask)])}, device_id_type=MESH)

        def received(self, g, mask, rounds):
            value = 0.0
            for b in orders[g][:rounds]:
                self.copy(g, b + mask).wait_recv()
                value += self.dst[b + mask, band(g)].astype(jnp.float32)
            return value

        def round(self, r):
            for mask in masks:
                for g in range(groups):
                    if turn(g, mask) == r:
                        value = self.share(g, mask)
                        self.src[mask, band(g)] = (value + self.received(g, mask, r)).astype(jnp.bfloat16)
                        self.copy(g, mask).start()

        def drain(self):
            for mask in masks:
                for g in range(groups):
                    self.copy(g, mask).wait_send()

    def share_end(g, mask):
        block = imgs[pl.ds(2 * chip, 2), :, part_of(mask)].reshape(2 * rows, cols)
        return jnp.dot(post_end[band(g)], block, preferred_element_type=jnp.float32)

    reduce_end = Reduction(sbuf_end, rbuf_end, ers_send, ers_recv, share_end)

    def row_of(column):
        return jnp.transpose(jnp.broadcast_to(column, (tpl_rows, 128)))[0:8]

    def hand_occ():
        return pltpu.make_async_remote_copy(
            src_ref=obuf_end, dst_ref=orecv_end, send_sem=hand_send.at[0],
            recv_sem=hand_recv.at[0], device_id={"tpl": outer}, device_id_type=MESH)

    def hand_evidence(q):
        return pltpu.make_async_remote_copy(
            src_ref=le_row.at[q], dst_ref=le_row.at[q], send_sem=hand_send.at[1],
            recv_sem=hand_recv.at[1], device_id={"tpl": outer}, device_id_type=MESH)

    def hand_sum(g):
        return pltpu.make_async_remote_copy(
            src_ref=zsend.at[band(g)], dst_ref=zrecv.at[band(g)], send_sem=z_send.at[g],
            recv_sem=z_recv.at[g], device_id={"tpl": outer}, device_id_type=MESH)

    def hub_spread(k):
        end_arrival(me_i, k).wait_recv()
        for off in masks:
            spread_copy(off, k).start()

    def hub_score():
        for off in range(1, n_img):
            for k in range(t_parts):
                end_arrival(img_peer(off), k).wait_recv()
        sqn_end[...] = half_norm(et_ref)
        end_score(chip)
        st[chip, end_slot, 0:1, :] = there[0]
        st[chip, end_slot, 1:2, :] = there[1]
        tell(chip, end_slot, est_send)

    def hub_consume():
        top, total = consume(chip)
        post = weigh(e_end, there[0], top, total)
        obuf_end[...] = row_of(jnp.sum(post, axis=1, keepdims=True))
        post_end[...] = post.astype(jnp.bfloat16)
        reduce_end.round(0)
        hand_occ().start()
        hand_evidence(chip).start()

    def middle(q, carry):
        @pl.when(jnp.logical_not(jnp.logical_or(absent(q, chip), is_hub & (q == chip))))
        def _():
            consume(q)

        @pl.when(jnp.logical_not(absent(q, chip)))
        def _():
            for j in range(n_img):
                part = slice(j * cols, (j + 1) * cols)
                block = imgs[pl.ds(2 * q, 2), :, part].reshape(2 * rows, cols)
                acc[:, part] += jnp.dot(post_ref[q], block, preferred_element_type=jnp.float32)

        return carry

    def middles():
        lax.fori_loop(1, chips - 1, middle, 0)

    finish(chip)
    n_far = last - rank - skip
    late = parts // 2 if hubs else 0

    def arrive(b, carry):
        q_far = chip + inward * (b + 1 + skip)

        def near_event(block, k):
            q_near = chip - inward * (block + 1)
            there = jnp.logical_and(block >= 0, block < rank)

            @pl.when(there)
            def _():
                relay(q_near, k, last > 0, 0, inner)

            if k == parts - 1:
                @pl.when(there)
                def _():
                    finish(q_near)

        for k in range(parts):
            @pl.when(b < n_far)
            def _():
                relay(q_far, k, rank > 0, 1, outer)

            if split and ready(k):
                @pl.when(jnp.logical_or(is_end, is_hub) & (b < n_far) & (q_far == opposite))
                def _():
                    finish_ahead(q_far)

            if k >= late:
                near_event(b, k - late)
            else:
                near_event(b - 1, k - late + parts)
            if hubs:
                spreads = [j for j in range(t_parts) if k == min(2 * j, parts - 1)]
                if spreads:
                    @pl.when(jnp.logical_and(is_hub, b == 0))
                    def _():
                        for j in spreads:
                            hub_spread(j)

                if k == parts // 2:
                    @pl.when(jnp.logical_and(is_end, b == n_far - 1))
                    def _():
                        middles()

                steps = ((parts // 3 - 1, hub_score), (parts // 2, hub_consume))
                due = [step for at, step in steps if k == max(0, min(at, parts - 1))]
                if due:
                    @pl.when(jnp.logical_and(is_hub, b == 1))
                    def _():
                        for step in due:
                            step()

        speaks = jnp.logical_or(is_end, is_hub) & (q_far == opposite)

        @pl.when(jnp.logical_and(b < n_far, jnp.logical_not(speaks)))
        def _():
            finish(q_far)

        if hubs:
            @pl.when(jnp.logical_and(b < n_far, speaks))
            def _():
                finish_last(q_far)

        return carry

    lax.fori_loop(0, last - 1 if hubs else last, arrive, 0)

    if hubs:
        @pl.when(is_hub)
        def _():
            for r in range(1, len(bits)):
                reduce_end.round(r)
            for g in range(groups):
                own_end[band(g)] = share_end(g, 0)

    @pl.when(jnp.logical_not(is_end))
    def _():
        middles()

    ends = (0, chips - 1) if chips > 1 else (0,)
    factors = {}
    for q in ends:
        top, total = gather_stats(q)
        factors[q] = jnp.exp(here[q, 0] - top) / total
    weighed = []

    def occ_copy(off):
        return pltpu.make_async_remote_copy(
            src_ref=obuf, dst_ref=orecv.at[off], send_sem=oc_send.at[off],
            recv_sem=oc_recv.at[off], device_id={"img": img_peer(off)}, device_id_type=MESH)

    def share(g, mask):
        if g not in weighed:
            weighed.append(g)
            for q in ends:
                post = e_ref[q, band(g)] * factors[q]
                post_ref[q, band(g)] = post.astype(jnp.bfloat16)
                e_ref[q, band(g)] = post
        part = part_of(mask)
        value = acc[band(g), part]
        for q in ends:
            block = imgs[2 * q:2 * q + 2, :, part].reshape(2 * rows, cols)
            value += jnp.dot(post_ref[q, band(g)], block, preferred_element_type=jnp.float32)
        return value

    reduce_own = Reduction(sbuf, rbuf, rs_send, rs_recv, share)
    mine = part_of(0)
    for r in range(len(bits)):
        reduce_own.round(r)
        if r == 0:
            for q in ends:
                occ[...] += jnp.sum(e_ref[q], axis=1, keepdims=True)
            obuf[...] = row_of(occ[...])
            if hubs:
                @pl.when(is_end)
                def _():
                    hand_occ().wait_recv()
                    hand_evidence(chip + inward).wait_recv()
                    obuf[...] += orecv_end[...]

            for off in range(1, n_img):
                occ_copy(off).start()
            for q in range(chips):
                le_ref[:, q * pair:(q + 1) * pair] = le_row[q]
            if hubs:
                @pl.when(is_hub)
                def _():
                    for g in range(groups):
                        zsend[band(g)] = (own_end[band(g)] + reduce_end.received(g, 0, len(bits))).astype(jnp.bfloat16)
                        hand_sum(g).start()

            for g in range(groups):
                own[band(g)] = share(g, 0) + t_ref[band(g), mine].astype(jnp.float32)
    if hubs:
        @pl.when(is_end)
        def _():
            for k in range(t_parts):
                end_copy(k).wait_send()

        @pl.when(is_hub)
        def _():
            for off in range(1, n_img):
                for k in range(t_parts):
                    spread_copy(off, k).wait_send()
            told(chip, end_slot, est_send)
            hand_occ().wait_send()
            hand_evidence(chip).wait_send()
            reduce_end.drain()

    def drain(q, carry):
        block = 2 * q + core
        away = (q - chip) * inward
        goes_out = (rank > 0) & (away >= 0) & jnp.logical_not(is_hub & (away == 0))
        for k in range(parts):
            @pl.when((away <= 0) & (last > 0))
            def _():
                image_copy(imgs.at[block], block, k, 0, inner).wait_send()

            @pl.when(goes_out)
            def _():
                image_copy(imgs.at[block], block, k, 1, outer).wait_send()

            @pl.when(jnp.logical_not(absent(q, chip)))
            def _():
                image_copy(imgs.at[block], block, k, 2, sibling).wait_send()

        @pl.when(jnp.logical_not(jnp.logical_or(absent(q, chip), is_end & (q == opposite))))
        def _():
            told(q, me_t, st_send)

        return carry

    lax.fori_loop(0, chips, drain, 0)

    occ_row = obuf[...]
    for off in range(1, n_img):
        occ_copy(off).wait_recv()
        occ_row += orecv[off]
    occ_col = jnp.transpose(jnp.broadcast_to(occ_row[0:1], (128, tpl_rows)))[:, 0:1]
    occ[...] = occ_col + 1.0

    if hubs:
        @pl.when(is_end)
        def _():
            for g in range(groups):
                hand_sum(g).wait_recv()
                own[band(g)] += zrecv[band(g)].astype(jnp.float32)

    for g in range(groups):
        out_ref[band(g)] = (own[band(g)] + reduce_own.received(g, 0, len(bits))) / occ[band(g)]

    for off in range(1, n_img):
        occ_copy(off).wait_send()
    reduce_own.drain()
    if hubs:
        @pl.when(is_hub)
        def _():
            for g in range(groups):
                hand_sum(g).wait_send()


def emit(new_ref, evidence_ref, new_out, evidence_out, sem):
    move = pltpu.make_async_copy(new_ref, new_out, sem)
    move.start()
    evidence_out[...] = evidence_ref[...].reshape(evidence_out.shape)
    move.wait()


def solution(mesh):
    n_img, n_tpl = mesh.shape["img"], mesh.shape["tpl"]
    chips = n_tpl // 2

    def per_device(images, templates, class_exponent, class_mask):
        rows, feats = images.shape
        tpl_rows = templates.shape[0]
        cols = feats // n_img
        class_count = class_exponent.shape[0]
        parts = max(c for c in (6, 3, 2, 1) if rows % (16 * c) == 0 or c == 1)
        dma = pltpu.SemaphoreType.DMA
        vmem = pl.BlockSpec(memory_space=pltpu.VMEM)
        far = pl.BlockSpec(memory_space=pl.ANY)
        new, evidence = pl.pallas_call(
            functools.partial(kernel, n_img, n_tpl, parts),
            out_shape=(
                pltpu.VMEM((tpl_rows, cols), jnp.float32),
                pltpu.VMEM((1, n_tpl * rows), jnp.float32),
            ),
            in_specs=[far, far, pl.BlockSpec(memory_space=pltpu.SMEM), far],
            out_specs=(vmem, vmem),
            scratch_shapes=[
                pltpu.VMEM((tpl_rows, feats), jnp.bfloat16),
                pltpu.VMEM((class_count, n_tpl * rows), jnp.int32),
                dma((3,)),
                pltpu.VMEM((n_tpl, rows, feats), jnp.bfloat16),
                pltpu.VMEM((chips, class_count, 2 * rows), jnp.int32),
                pltpu.VMEM((chips, 1, 2 * rows), jnp.float32),
                pltpu.VMEM((chips, tpl_rows, 2 * rows), jnp.float32),
                pltpu.VMEM((chips, tpl_rows, 2 * rows), jnp.bfloat16),
                pltpu.VMEM((chips, n_tpl, 2, 2 * rows), jnp.float32),
                pltpu.VMEM((tpl_rows, feats), jnp.float32),
                pltpu.VMEM((tpl_rows, cols), jnp.float32),
                pltpu.VMEM((n_img, tpl_rows, cols), jnp.bfloat16),
                pltpu.VMEM((n_img, tpl_rows, cols), jnp.bfloat16),
                pltpu.VMEM((tpl_rows, 1), jnp.float32),
                pltpu.VMEM((tpl_rows, 1), jnp.float32),
                pltpu.VMEM((8, tpl_rows), jnp.float32),
                pltpu.VMEM((n_img, 8, tpl_rows), jnp.float32),
                dma((3, chips, parts)),
                dma((n_tpl, parts)),
                dma((chips, n_tpl)),
                dma((chips, n_tpl)),
                dma((n_img, n_img)),
                dma((n_img, n_img)),
                dma((n_img,)),
                dma((n_img,)),
                pltpu.VMEM((chips, 2, 1, 2 * rows), jnp.float32),
                pltpu.VMEM((2, 1, 2 * rows), jnp.float32),
                pltpu.VMEM((tpl_rows, feats), jnp.bfloat16),
                pltpu.VMEM((tpl_rows, 2 * rows), jnp.float32),
                pltpu.VMEM((tpl_rows, 2 * rows), jnp.bfloat16),
                pltpu.VMEM((tpl_rows, 1), jnp.float32),
                pltpu.VMEM((tpl_rows, 1), jnp.float32),
                pltpu.VMEM((tpl_rows, cols), jnp.float32),
                pltpu.VMEM((n_img, tpl_rows, cols), jnp.bfloat16),
                pltpu.VMEM((n_img, tpl_rows, cols), jnp.bfloat16),
                pltpu.VMEM((tpl_rows, cols), jnp.bfloat16),
                pltpu.VMEM((tpl_rows, cols), jnp.bfloat16),
                pltpu.VMEM((8, tpl_rows), jnp.float32),
                pltpu.VMEM((8, tpl_rows), jnp.float32),
                dma((n_img, 2)),
                dma((n_img, 2)),
                dma((chips, n_tpl)),
                dma((n_img, n_img)),
                dma((n_img, n_img)),
                dma((n_img,)),
                dma((n_img,)),
                dma((2,)),
                dma((2,)),
            ],
            compiler_params=pltpu.CompilerParams(
                collective_id=0, has_side_effects=True, vmem_limit_bytes=60 * 1024 * 1024),
        )(images, templates, class_exponent, class_mask.T)
        return pl.pallas_call(
            emit,
            out_shape=(
                jax.ShapeDtypeStruct(new.shape, jnp.float32),
                jax.ShapeDtypeStruct((n_tpl * rows,), jnp.float32),
            ),
            in_specs=[vmem] * 2,
            out_specs=(far, vmem),
            scratch_shapes=[dma],
        )(*[pltpu.with_memory_space_constraint(x, pltpu.VMEM) for x in (new, evidence)])

    in_specs = (P(("img", "tpl"), None), P("tpl", None), P(), P("img", None))
    out_specs = (P("tpl", "img"), P("img"))
    return jax.shard_map(
        per_device, mesh=mesh, in_specs=in_specs, out_specs=out_specs, check_vma=False
    )
```

```python
import functools

import jax
import jax.numpy as jnp
from jax import lax
from jax.experimental import pallas as pl
from jax.experimental.pallas import tpu as pltpu
from jax.sharding import PartitionSpec as P

MESH = pl.DeviceIdType.MESH
floor_score = -1e30


def kernel(
    n_img, n_tpl, parts, x_ref, t_hbm, power_ref, mask_hbm, out_ref, le_ref,
    t_ref, mask_ref, loads, imgs, allow, le_row, e_ref, post_ref, st, acc, own, sbuf, rbuf, sqn, occ, obuf, orecv,
    img_send, img_recv, st_send, st_recv, rs_send, rs_recv, oc_send, oc_recv,
    here, there, et_ref, e_end, post_end, sqn_end, occ_end, own_end, sbuf_end, rbuf_end, zsend, zrecv, obuf_end, orecv_end,
    et_send, et_recv, est_send, ers_send, ers_recv, z_send, z_recv, hand_send, hand_recv,
):
    chips = n_tpl // 2
    last = chips - 1
    hubs = chips >= 4
    rows, feats = x_ref.shape
    cols = feats // n_img
    me_i, me_t = lax.axis_index("img"), lax.axis_index("tpl")
    chip, core = lax.div(me_t, 2), lax.rem(me_t, 2)
    sibling = 2 * chip + 1 - core
    side = lax.div(2 * chip, chips)
    inward = 1 - 2 * side
    rank = chip + side * (last - 2 * chip)
    inner, outer = me_t + 2 * inward, me_t - 2 * inward
    is_end = jnp.logical_and(rank == 0, hubs)
    is_hub = jnp.logical_and(rank == 1, hubs)
    skip = jnp.where(is_end, 1, 0)
    end_slot = outer
    opposite = last * (1 - side)

    def absent(q, who):
        if not hubs:
            return False
        low = jnp.logical_and(q == 1, who == 0)
        return jnp.logical_or(low, jnp.logical_and(q == last - 1, who == last))

    def tpl_peer(off):
        return lax.rem(me_t + off, n_tpl)

    def img_peer(off):
        return lax.rem(me_i + off, n_img)

    barrier = pltpu.get_barrier_semaphore()
    for off in range(1, n_tpl):
        pl.semaphore_signal(barrier, inc=1, device_id={"tpl": tpl_peer(off)}, device_id_type=MESH)
    for off in range(1, n_img):
        pl.semaphore_signal(barrier, inc=1, device_id={"img": img_peer(off)}, device_id_type=MESH)
    load_t = pltpu.make_async_copy(t_hbm, t_ref, loads.at[0])
    load_x = pltpu.make_async_copy(x_ref, imgs.at[me_t], loads.at[1])
    load_mask = pltpu.make_async_copy(mask_hbm, mask_ref, loads.at[2])
    for load in (load_t, load_x, load_mask):
        load.start()
    pl.semaphore_wait(barrier, n_tpl - 1 + n_img - 1)

    size = rows // parts
    tpl_rows = t_ref.shape[0]
    quarter = tpl_rows // n_img
    t_parts = 2 if quarter % 32 == 0 else 1
    t_size = quarter // t_parts

    pair = 2 * rows
    ahead = 2 * rows // 3
    split = hubs and parts % 3 == 0 and ahead % 128 == 0 and pair == 3 * ahead
    early = ((0, ahead), (pair - ahead, pair)) if split else ()
    late_lanes = ((ahead, pair - ahead),) if split else ((0, pair),)

    def image_copy(src, block, k, way, to):
        place = k + lax.rem(block, 2) * (parts - 1 - 2 * k) if split else k
        piece = pl.ds(pl.multiple_of(place * size, size), size)
        return pltpu.make_async_remote_copy(
            src_ref=src.at[piece], dst_ref=imgs.at[block, piece],
            send_sem=img_send.at[way, lax.div(block, 2), k],
            recv_sem=img_recv.at[block, k], device_id={"tpl": to}, device_id_type=MESH)

    def share_rows(owner, k):
        return pl.ds(owner * quarter + k * t_size, t_size)

    def end_copy(k):
        piece = share_rows(me_i, k)
        return pltpu.make_async_remote_copy(
            src_ref=t_hbm.at[piece], dst_ref=et_ref.at[piece], send_sem=et_send.at[0, k],
            recv_sem=et_recv.at[me_i, k], device_id={"tpl": inner}, device_id_type=MESH)

    def spread_copy(off, k):
        piece = share_rows(me_i, k)
        return pltpu.make_async_remote_copy(
            src_ref=et_ref.at[piece], dst_ref=et_ref.at[piece], send_sem=et_send.at[off, k],
            recv_sem=et_recv.at[me_i, k], device_id={"img": flip(off)}, device_id_type=MESH)

    def end_arrival(owner, k):
        piece = share_rows(owner, k)
        return pltpu.make_async_remote_copy(
            src_ref=et_ref.at[piece], dst_ref=et_ref.at[piece], send_sem=et_send.at[0, k],
            recv_sem=et_recv.at[owner, k], device_id={"img": img_peer(1)}, device_id_type=MESH)

    own_block = 2 * chip + core
    sends_out = jnp.logical_and(rank > 0, jnp.logical_not(is_hub))
    if hubs:
        @pl.when(is_end)
        def _():
            for k in range(t_parts):
                end_copy(k).start()

    for k in range(parts):
        if chips > 1:
            image_copy(x_ref, own_block, k, 0, inner).start()

        @pl.when(sends_out)
        def _():
            image_copy(x_ref, own_block, k, 1, outer).start()

        image_copy(x_ref, own_block, k, 2, sibling).start()

    for load in (load_t, load_x, load_mask):
        load.wait()

    def half_norm(ref):
        tf = ref[...].astype(jnp.float32)
        return 0.5 * jnp.sum(tf * tf, axis=1, keepdims=True)

    sqn[...] = half_norm(t_ref)
    acc[...] = jnp.zeros_like(acc)
    occ[...] = jnp.zeros_like(occ)

    def stat_copy(q, slot, off, sems):
        return pltpu.make_async_remote_copy(
            src_ref=st.at[q, slot], dst_ref=st.at[q, slot], send_sem=sems.at[q, off],
            recv_sem=st_recv.at[q, slot], device_id={"tpl": tpl_peer(off)}, device_id_type=MESH)

    def stat_arrival(q, slot):
        return pltpu.make_async_remote_copy(
            src_ref=st.at[q, slot], dst_ref=st.at[q, slot], send_sem=st_send.at[q, 0],
            recv_sem=st_recv.at[q, slot], device_id={"tpl": tpl_peer(1)}, device_id_type=MESH)

    def tell(q, slot, sems):
        for off in sorted(range(1, n_tpl), key=lambda o: abs(o - n_tpl // 2)):
            @pl.when(jnp.logical_not(absent(q, lax.div(tpl_peer(off), 2))))
            def _():
                stat_copy(q, slot, off, sems).start()

    def told(q, slot, sems):
        for off in range(1, n_tpl):
            @pl.when(jnp.logical_not(absent(q, lax.div(tpl_peer(off), 2))))
            def _():
                stat_copy(q, slot, off, sems).wait_send()

    def pair_of(q):
        return imgs[pl.ds(2 * q, 2)].reshape(2 * rows, feats)

    def images_of(q, lanes):
        cuts = [(c, max(lo - c * rows, 0), min(hi - c * rows, rows)) for lo, hi in lanes for c in range(2)]
        return jnp.concatenate([imgs[2 * q + c, lo:hi] for c, lo, hi in cuts if lo < hi])

    class_count = power_ref.shape[0]
    per_class = tpl_rows * n_tpl // class_count
    for q in range(chips):
        allow[q] = mask_ref[:, q * pair:(q + 1) * pair]

    def inverse_temp(c):
        power = jnp.full((1, pair), power_ref[c], jnp.int32)
        return 0.5 * jnp.exp2(0.5 * power.astype(jnp.float32))

    def class_terms(slot, q, lanes):
        first = slot * tpl_rows
        width = sum(hi - lo for lo, hi in lanes)

        def mask_of(c):
            row = allow[q, pl.ds(c, 1), :]
            return jnp.concatenate([row[:, lo:hi] for lo, hi in lanes], axis=1)

        if per_class % tpl_rows == 0:
            only = lax.div(first, per_class)
            return inverse_temp(only)[:, :width], mask_of(only) > 0
        owner = lax.div(first + lax.broadcasted_iota(jnp.int32, (tpl_rows, width), 0), per_class)
        beta = sum(jnp.where(owner == c, inverse_temp(c)[:, :width], 0.0) for c in range(class_count))
        return beta, sum(jnp.where(owner == c, mask_of(c), 0) for c in range(class_count)) > 0

    def score(q, slot, tpl, norm, e_out, tops, totals, lanes=None):
        images = pair_of(q) if lanes is None else images_of(q, lanes)
        lanes = lanes or ((0, pair),)
        raw = lax.dot_general(
            tpl[...], images, (((1,), (1,)), ((), ())), preferred_element_type=jnp.float32)
        beta, allowed = class_terms(slot, q, lanes)
        s = beta * (raw - norm[...])
        top = jnp.max(jnp.where(allowed, s, floor_score), axis=0, keepdims=True)
        e = jnp.where(allowed, jnp.exp(s - top), 0.0)
        total = jnp.sum(e, axis=0, keepdims=True)
        at = 0
        for lo, hi in lanes:
            tops[:, lo:hi] = top[:, at:at + hi - lo]
            totals[:, lo:hi] = total[:, at:at + hi - lo]
            if e_out is not None:
                e_out[:, lo:hi] = e[:, at:at + hi - lo]
            at += hi - lo

    def own_score(q, lanes=None):
        score(q, me_t, t_ref, sqn, e_ref.at[q], here.at[q, 0], here.at[q, 1], lanes)

    def end_score(q, lanes=None):
        score(q, end_slot, et_ref, sqn_end, e_end if q is chip else None, there.at[0], there.at[1], lanes)

    def put_stats(q):
        st[q, me_t, 0:1, :] = here[q, 0]
        st[q, me_t, 1:2, :] = here[q, 1]

    def put_joint_stats(q):
        top = jnp.maximum(here[q, 0], there[0])
        st[q, me_t, 0:1, :] = top
        st[q, me_t, 1:2, :] = here[q, 1] * jnp.exp(here[q, 0] - top) + there[1] * jnp.exp(there[0] - top)

    def wait_image(block, k):
        image_copy(imgs.at[block], block, k, 2, sibling).wait_recv()

    def relay(q, k, more, way, to):
        block = 2 * q + core
        wait_image(block, k)

        image_copy(imgs.at[block], block, k, 2, sibling).start()

        @pl.when(more)
        def _():
            image_copy(imgs.at[block], block, k, way, to).start()

    def wait_sibling(q):
        for k in range(parts):
            wait_image(2 * q + 1 - core, k)

    def finish(q):
        wait_sibling(q)
        own_score(q)
        put_stats(q)
        tell(q, me_t, st_send)

    def ready(k):
        return k == 2 * parts // 3

    def finish_ahead(q):
        for k in range(2 * parts // 3):
            wait_image(2 * q + 1 - core, k)
        own_score(q, early)

        @pl.when(is_hub)
        def _():
            end_score(q, early)

    def finish_last(q):
        for k in range(2 * parts // 3 if split else 0, parts):
            wait_image(2 * q + 1 - core, k)
        own_score(q, late_lanes)

        @pl.when(is_hub)
        def _():
            end_score(q, late_lanes)
            put_joint_stats(q)
            tell(q, me_t, st_send)

    def mute(q, who):
        if not hubs:
            return False
        low = jnp.logical_and(q == last, who == 0)
        return jnp.logical_or(low, jnp.logical_and(q == 0, who == last))

    def gather_stats(q):
        for off in range(1, n_tpl):
            slot = tpl_peer(off)
            silent = jnp.logical_or(is_hub & (q == chip) & (slot == end_slot), mute(q, lax.div(slot, 2)))

            @pl.when(jnp.logical_not(silent))
            def _():
                stat_arrival(q, slot).wait_recv()

        heard = range(n_tpl)
        if hubs and isinstance(q, int):
            heard = [j for j in heard if not (q == last and j < 2) and not (q == 0 and j >= 2 * last)]
        tops = {j: st[q, j, 0:1, :] for j in heard}
        top = functools.reduce(jnp.maximum, tops.values())
        total = sum(st[q, j, 1:2, :] * jnp.exp(tops[j] - top) for j in heard)
        le_row[q] = top + jnp.log(total)
        return top, total

    def weigh(e, local, top, total):
        return e[...] * (jnp.exp(local - top) / total)

    def consume(q):
        top, total = gather_stats(q)
        post = weigh(e_ref.at[q], here[q, 0], top, total)
        post_ref[q] = post.astype(jnp.bfloat16)
        occ[...] += jnp.sum(post, axis=1, keepdims=True)
        return top, total

    bits = [1 << k for k in range(n_img.bit_length() - 1)]
    groups = len(bits) if bits and tpl_rows % (16 * len(bits)) == 0 else 1
    depth = tpl_rows // groups
    orders = [bits[g:] + bits[:g] for g in range(groups)]
    masks = sorted(range(1, n_img), key=lambda mask: -mask.bit_count())

    def flip(mask):
        return me_i + sum(b - 2 * b * lax.rem(lax.div(me_i, b), 2) for b in bits if b & mask)

    def turn(g, mask):
        return next(r for r, b in enumerate(orders[g]) if b & mask)

    def band(g):
        return slice(g * depth, (g + 1) * depth)

    def part_of(mask):
        return pl.ds(pl.multiple_of(flip(mask) * cols, cols), cols)

    class Reduction:
        def __init__(self, src, dst, sent, got, share):
            self.src, self.dst, self.sent, self.got, self.share = src, dst, sent, got, share

        def copy(self, g, mask):
            return pltpu.make_async_remote_copy(
                src_ref=self.src.at[mask, band(g)], dst_ref=self.dst.at[mask, band(g)],
                send_sem=self.sent.at[g, mask], recv_sem=self.got.at[g, mask],
                device_id={"img": flip(orders[g][turn(g, mask)])}, device_id_type=MESH)

        def received(self, g, mask, rounds):
            value = 0.0
            for b in orders[g][:rounds]:
                self.copy(g, b + mask).wait_recv()
                value += self.dst[b + mask, band(g)].astype(jnp.float32)
            return value

        def round(self, r):
            for mask in masks:
                for g in range(groups):
                    if turn(g, mask) == r:
                        value = self.share(g, mask)
                        self.src[mask, band(g)] = (value + self.received(g, mask, r)).astype(jnp.bfloat16)
                        self.copy(g, mask).start()

        def drain(self):
            for mask in masks:
                for g in range(groups):
                    self.copy(g, mask).wait_send()

    def share_end(g, mask):
        block = imgs[pl.ds(2 * chip, 2), :, part_of(mask)].reshape(2 * rows, cols)
        return jnp.dot(post_end[band(g)], block, preferred_element_type=jnp.float32)

    reduce_end = Reduction(sbuf_end, rbuf_end, ers_send, ers_recv, share_end)

    def row_of(column):
        return jnp.transpose(jnp.broadcast_to(column, (tpl_rows, 128)))[0:8]

    def hand_occ():
        return pltpu.make_async_remote_copy(
            src_ref=obuf_end, dst_ref=orecv_end, send_sem=hand_send.at[0],
            recv_sem=hand_recv.at[0], device_id={"tpl": outer}, device_id_type=MESH)

    def hand_evidence(q):
        return pltpu.make_async_remote_copy(
            src_ref=le_row.at[q], dst_ref=le_row.at[q], send_sem=hand_send.at[1],
            recv_sem=hand_recv.at[1], device_id={"tpl": outer}, device_id_type=MESH)

    def hand_sum(g):
        return pltpu.make_async_remote_copy(
            src_ref=zsend.at[band(g)], dst_ref=zrecv.at[band(g)], send_sem=z_send.at[g],
            recv_sem=z_recv.at[g], device_id={"tpl": outer}, device_id_type=MESH)

    def hub_spread(k):
        end_arrival(me_i, k).wait_recv()
        for off in masks:
            spread_copy(off, k).start()

    def hub_score():
        for off in range(1, n_img):
            for k in range(t_parts):
                end_arrival(img_peer(off), k).wait_recv()
        sqn_end[...] = half_norm(et_ref)
        end_score(chip)
        st[chip, end_slot, 0:1, :] = there[0]
        st[chip, end_slot, 1:2, :] = there[1]
        tell(chip, end_slot, est_send)

    def hub_consume():
        top, total = consume(chip)
        post = weigh(e_end, there[0], top, total)
        obuf_end[...] = row_of(jnp.sum(post, axis=1, keepdims=True))
        post_end[...] = post.astype(jnp.bfloat16)
        reduce_end.round(0)
        hand_occ().start()
        hand_evidence(chip).start()

    def middle(q, carry):
        @pl.when(jnp.logical_not(jnp.logical_or(absent(q, chip), is_hub & (q == chip))))
        def _():
            consume(q)

        @pl.when(jnp.logical_not(absent(q, chip)))
        def _():
            for j in range(n_img):
                part = slice(j * cols, (j + 1) * cols)
                block = imgs[pl.ds(2 * q, 2), :, part].reshape(2 * rows, cols)
                acc[:, part] += jnp.dot(post_ref[q], block, preferred_element_type=jnp.float32)

        return carry

    def middles():
        lax.fori_loop(1, chips - 1, middle, 0)

    finish(chip)
    n_far = last - rank - skip
    late = parts // 2 if hubs else 0

    def arrive(b, carry):
        q_far = chip + inward * (b + 1 + skip)

        def near_event(block, k):
            q_near = chip - inward * (block + 1)
            there = jnp.logical_and(block >= 0, block < rank)

            @pl.when(there)
            def _():
                relay(q_near, k, last > 0, 0, inner)

            if k == parts - 1:
                @pl.when(there)
                def _():
                    finish(q_near)

        for k in range(parts):
            @pl.when(b < n_far)
            def _():
                relay(q_far, k, rank > 0, 1, outer)

            if split and ready(k):
                @pl.when(jnp.logical_or(is_end, is_hub) & (b < n_far) & (q_far == opposite))
                def _():
                    finish_ahead(q_far)

            if k >= late:
                near_event(b, k - late)
            else:
                near_event(b - 1, k - late + parts)
            if hubs:
                spreads = [j for j in range(t_parts) if k == min(2 * j, parts - 1)]
                if spreads:
                    @pl.when(jnp.logical_and(is_hub, b == 0))
                    def _():
                        for j in spreads:
                            hub_spread(j)

                if k == parts // 2:
                    @pl.when(jnp.logical_and(is_end, b == n_far - 1))
                    def _():
                        middles()

                steps = ((parts // 3 - 1, hub_score), (parts // 2, hub_consume))
                due = [step for at, step in steps if k == max(0, min(at, parts - 1))]
                if due:
                    @pl.when(jnp.logical_and(is_hub, b == 1))
                    def _():
                        for step in due:
                            step()

        speaks = jnp.logical_or(is_end, is_hub) & (q_far == opposite)

        @pl.when(jnp.logical_and(b < n_far, jnp.logical_not(speaks)))
        def _():
            finish(q_far)

        if hubs:
            @pl.when(jnp.logical_and(b < n_far, speaks))
            def _():
                finish_last(q_far)

        return carry

    lax.fori_loop(0, last - 1 if hubs else last, arrive, 0)

    if hubs:
        @pl.when(is_hub)
        def _():
            for r in range(1, len(bits)):
                reduce_end.round(r)
            for g in range(groups):
                own_end[band(g)] = share_end(g, 0)

    @pl.when(jnp.logical_not(is_end))
    def _():
        middles()

    ends = (0, chips - 1) if chips > 1 else (0,)
    factors = {}
    for q in ends:
        top, total = gather_stats(q)
        factors[q] = jnp.exp(here[q, 0] - top) / total
    weighed = []

    def occ_copy(off):
        return pltpu.make_async_remote_copy(
            src_ref=obuf, dst_ref=orecv.at[off], send_sem=oc_send.at[off],
            recv_sem=oc_recv.at[off], device_id={"img": img_peer(off)}, device_id_type=MESH)

    def share(g, mask):
        if g not in weighed:
            weighed.append(g)
            for q in ends:
                post = e_ref[q, band(g)] * factors[q]
                post_ref[q, band(g)] = post.astype(jnp.bfloat16)
                e_ref[q, band(g)] = post
        part = part_of(mask)
        value = acc[band(g), part]
        for q in ends:
            block = imgs[2 * q:2 * q + 2, :, part].reshape(2 * rows, cols)
            value += jnp.dot(post_ref[q, band(g)], block, preferred_element_type=jnp.float32)
        return value

    reduce_own = Reduction(sbuf, rbuf, rs_send, rs_recv, share)
    mine = part_of(0)
    for r in range(len(bits)):
        reduce_own.round(r)
        if r == 0:
            for q in ends:
                occ[...] += jnp.sum(e_ref[q], axis=1, keepdims=True)
            obuf[...] = row_of(occ[...])
            if hubs:
                @pl.when(is_end)
                def _():
                    hand_occ().wait_recv()
                    hand_evidence(chip + inward).wait_recv()
                    obuf[...] += orecv_end[...]

            for off in range(1, n_img):
                occ_copy(off).start()
            for q in range(chips):
                le_ref[:, q * pair:(q + 1) * pair] = le_row[q]
            if hubs:
                @pl.when(is_hub)
                def _():
                    for g in range(groups):
                        zsend[band(g)] = (own_end[band(g)] + reduce_end.received(g, 0, len(bits))).astype(jnp.bfloat16)
                        hand_sum(g).start()

            for g in range(groups):
                own[band(g)] = share(g, 0) + t_ref[band(g), mine].astype(jnp.float32)
    if hubs:
        @pl.when(is_end)
        def _():
            for k in range(t_parts):
                end_copy(k).wait_send()

        @pl.when(is_hub)
        def _():
            for off in range(1, n_img):
                for k in range(t_parts):
                    spread_copy(off, k).wait_send()
            told(chip, end_slot, est_send)
            hand_occ().wait_send()
            hand_evidence(chip).wait_send()
            reduce_end.drain()

    def drain(q, carry):
        block = 2 * q + core
        away = (q - chip) * inward
        goes_out = (rank > 0) & (away >= 0) & jnp.logical_not(is_hub & (away == 0))
        for k in range(parts):
            @pl.when((away <= 0) & (last > 0))
            def _():
                image_copy(imgs.at[block], block, k, 0, inner).wait_send()

            @pl.when(goes_out)
            def _():
                image_copy(imgs.at[block], block, k, 1, outer).wait_send()

            @pl.when(jnp.logical_not(absent(q, chip)))
            def _():
                image_copy(imgs.at[block], block, k, 2, sibling).wait_send()

        @pl.when(jnp.logical_not(jnp.logical_or(absent(q, chip), is_end & (q == opposite))))
        def _():
            told(q, me_t, st_send)

        return carry

    lax.fori_loop(0, chips, drain, 0)

    occ_row = obuf[...]
    for off in range(1, n_img):
        occ_copy(off).wait_recv()
        occ_row += orecv[off]
    occ_col = jnp.transpose(jnp.broadcast_to(occ_row[0:1], (128, tpl_rows)))[:, 0:1]
    occ[...] = occ_col + 1.0

    if hubs:
        @pl.when(is_end)
        def _():
            for g in range(groups):
                hand_sum(g).wait_recv()
                own[band(g)] += zrecv[band(g)].astype(jnp.float32)

    for g in range(groups):
        out_ref[band(g)] = (own[band(g)] + reduce_own.received(g, 0, len(bits))) / occ[band(g)]

    for off in range(1, n_img):
        occ_copy(off).wait_send()
    reduce_own.drain()
    if hubs:
        @pl.when(is_hub)
        def _():
            for g in range(groups):
                hand_sum(g).wait_send()


def emit(new_ref, evidence_ref, new_out, evidence_out, sem):
    move = pltpu.make_async_copy(new_ref, new_out, sem)
    move.start()
    evidence_out[...] = evidence_ref[...].reshape(evidence_out.shape)
    move.wait()


def solution(mesh):
    n_img, n_tpl = mesh.shape["img"], mesh.shape["tpl"]
    chips = n_tpl // 2

    def per_device(images, templates, class_exponent, class_mask):
        rows, feats = images.shape
        tpl_rows = templates.shape[0]
        cols = feats // n_img
        class_count = class_exponent.shape[0]
        parts = max(c for c in (6, 3, 2, 1) if rows % (16 * c) == 0 or c == 1)
        dma = pltpu.SemaphoreType.DMA
        vmem = pl.BlockSpec(memory_space=pltpu.VMEM)
        far = pl.BlockSpec(memory_space=pl.ANY)
        new, evidence = pl.pallas_call(
            functools.partial(kernel, n_img, n_tpl, parts),
            out_shape=(
                pltpu.VMEM((tpl_rows, cols), jnp.float32),
                pltpu.VMEM((1, n_tpl * rows), jnp.float32),
            ),
            in_specs=[far, far, pl.BlockSpec(memory_space=pltpu.SMEM), far],
            out_specs=(vmem, vmem),
            scratch_shapes=[
                pltpu.VMEM((tpl_rows, feats), jnp.bfloat16),
                pltpu.VMEM((class_count, n_tpl * rows), jnp.int32),
                dma((3,)),
                pltpu.VMEM((n_tpl, rows, feats), jnp.bfloat16),
                pltpu.VMEM((chips, class_count, 2 * rows), jnp.int32),
                pltpu.VMEM((chips, 1, 2 * rows), jnp.float32),
                pltpu.VMEM((chips, tpl_rows, 2 * rows), jnp.float32),
                pltpu.VMEM((chips, tpl_rows, 2 * rows), jnp.bfloat16),
                pltpu.VMEM((chips, n_tpl, 2, 2 * rows), jnp.float32),
                pltpu.VMEM((tpl_rows, feats), jnp.float32),
                pltpu.VMEM((tpl_rows, cols), jnp.float32),
                pltpu.VMEM((n_img, tpl_rows, cols), jnp.bfloat16),
                pltpu.VMEM((n_img, tpl_rows, cols), jnp.bfloat16),
                pltpu.VMEM((tpl_rows, 1), jnp.float32),
                pltpu.VMEM((tpl_rows, 1), jnp.float32),
                pltpu.VMEM((8, tpl_rows), jnp.float32),
                pltpu.VMEM((n_img, 8, tpl_rows), jnp.float32),
                dma((3, chips, parts)),
                dma((n_tpl, parts)),
                dma((chips, n_tpl)),
                dma((chips, n_tpl)),
                dma((n_img, n_img)),
                dma((n_img, n_img)),
                dma((n_img,)),
                dma((n_img,)),
                pltpu.VMEM((chips, 2, 1, 2 * rows), jnp.float32),
                pltpu.VMEM((2, 1, 2 * rows), jnp.float32),
                pltpu.VMEM((tpl_rows, feats), jnp.bfloat16),
                pltpu.VMEM((tpl_rows, 2 * rows), jnp.float32),
                pltpu.VMEM((tpl_rows, 2 * rows), jnp.bfloat16),
                pltpu.VMEM((tpl_rows, 1), jnp.float32),
                pltpu.VMEM((tpl_rows, 1), jnp.float32),
                pltpu.VMEM((tpl_rows, cols), jnp.float32),
                pltpu.VMEM((n_img, tpl_rows, cols), jnp.bfloat16),
                pltpu.VMEM((n_img, tpl_rows, cols), jnp.bfloat16),
                pltpu.VMEM((tpl_rows, cols), jnp.bfloat16),
                pltpu.VMEM((tpl_rows, cols), jnp.bfloat16),
                pltpu.VMEM((8, tpl_rows), jnp.float32),
                pltpu.VMEM((8, tpl_rows), jnp.float32),
                dma((n_img, 2)),
                dma((n_img, 2)),
                dma((chips, n_tpl)),
                dma((n_img, n_img)),
                dma((n_img, n_img)),
                dma((n_img,)),
                dma((n_img,)),
                dma((2,)),
                dma((2,)),
            ],
            compiler_params=pltpu.CompilerParams(
                collective_id=0, has_side_effects=True, vmem_limit_bytes=60 * 1024 * 1024),
        )(images, templates, class_exponent, class_mask.T)
        return pl.pallas_call(
            emit,
            out_shape=(
                jax.ShapeDtypeStruct(new.shape, jnp.float32),
                jax.ShapeDtypeStruct((n_tpl * rows,), jnp.float32),
            ),
            in_specs=[vmem] * 2,
            out_specs=(far, vmem),
            scratch_shapes=[dma],
        )(*[pltpu.with_memory_space_constraint(x, pltpu.VMEM) for x in (new, evidence)])

    in_specs = (P(("img", "tpl"), None), P("tpl", None), P(), P("img", None))
    out_specs = (P("tpl", "img"), P("img"))
    return jax.shard_map(
        per_device, mesh=mesh, in_specs=in_specs, out_specs=out_specs, check_vma=False
    )
```
